512 devices in a mesh: gx: 32 (over x, z_hi, core), gy: 16 (over y, z_lo).
Axes of the slice: x: 4, y: 4, z: 16 (z_hi: 4, z_lo: 4; z = z_hi * 4 + z_lo), core: 2. Of those that a mesh axis runs over, the one named last changes fastest.
Arguments:
- populations: float32 [19, 256, 256, 128], P(None, 'gx', 'gy'), may hold values from 0.02 to 0.1
- solid: int32 [256, 256, 128], P('gx', 'gy'), may hold values 0 or 1
- visible: int32 [16, 16, 8], replicated, may hold values 0 or 1
- omega: float32 [1], replicated, may hold values from 1 to 1.6
- iso_levels: float32 [8], replicated, may hold values from -1 to 1
- iso_index: int32 [16, 16], replicated, may hold values from 0 to 7
Outputs:
- new_populations: float32 [19, 256, 256, 128], P(None, 'gx', 'gy')
- q_field: float32 [256, 256, 128], P('gx', 'gy')
- crossings: float32 [3, 256, 256, 128], P(None, 'gx', 'gy')
The draws below stay inside these ranges and needn't reach their ends.
All inputs are finite; a program needn't handle non-finite values. No bound on the sum of `solid` on one device may be relied on, other than what follows from the above.
Results may differ from the reference program's by a relative error of at most 0.000033.
Values sent between devices are 32-bit elements; how exact they have to be, the bound alone decides.
No kernel may reach another device: no remote copies, remote signals or barrier semaphores. Data moves between devices by JAX's collectives and lax.ppermute only.
A program may use at most 64 MiB of HBM per device.

```python
import jax
import jax.numpy as jnp

Q = 19
BRICK = 16
LEVELS = 8
NZ = 128
NX = 256
NY = 256


def touch_ends(values, rng, low, top_value):
    index_at = [jax.random.randint(jax.random.fold_in(rng, axis), (), 0, length) for axis, length in enumerate(values.shape)]
    widest = values.shape.index(max(values.shape))
    neighbour = index_at[:widest] + [(index_at[widest] + 1) % values.shape[widest]] + index_at[widest + 1:]
    return values.at[tuple(index_at)].set(low).at[tuple(neighbour)].set(top_value)


def block_levels(stream_key, extent, pieces, smallest, high):
    factor_of, own = 1.0, jax.random.fold_in(stream_key, 6)
    for position, blocks in pieces:
        steps = jnp.exp(jax.random.uniform(jax.random.fold_in(own, position), (blocks,), jnp.float32, smallest / len(pieces), high / len(pieces)))
        factor_of = factor_of * jnp.repeat(steps, extent[position] // blocks).reshape([-1 if axis == position else 1 for axis in range(len(extent))])
    return factor_of


def setup_inputs(seed: int = 0) -> dict:
    key_list = jax.random.split(jax.random.key(seed), 7)
    populations = jnp.clip(0.02 + 0.08 * jax.random.uniform(key_list[0], (Q, NX, NY, NZ), jnp.float32) ** block_levels(key_list[0], (Q, NX, NY, NZ), ((1, 32), (2, 16)), -0.2, 0.2), 0.02, 0.1)
    solid = touch_ends((jax.random.randint(key_list[1], (NX, NY, NZ), 0, 8) < 1).astype(jnp.int32), jax.random.fold_in(key_list[1], 1), 0, 1)
    visible = touch_ends((jax.random.randint(key_list[2], (NX // BRICK, NY // BRICK, NZ // BRICK), 0, 3) < 1).astype(jnp.int32), jax.random.fold_in(key_list[2], 1), 0, 1)
    omega = jnp.clip(jax.random.uniform(key_list[3], (1,), jnp.float32, 1.0, 1.6), 1.0, 1.6)
    iso_levels = jnp.clip(jax.random.uniform(key_list[4], (LEVELS,), jnp.float32, -1.0, 1.0), -1.0, 1.0)
    iso_index = touch_ends(jax.random.randint(key_list[5], (NX // BRICK, NY // BRICK), 0, LEVELS), jax.random.fold_in(key_list[5], 1), 0, LEVELS - 1).astype(jnp.int32)
    return {"populations": populations, "solid": solid, "visible": visible, "omega": omega, "iso_levels": iso_levels, "iso_index": iso_index}


LATTICE = [(0, 0, 0), (1, 0, 0), (-1, 0, 0), (0, 1, 0), (0, -1, 0), (0, 0, 1), (0, 0, -1),
           (1, 1, 0), (-1, -1, 0), (1, -1, 0), (-1, 1, 0), (1, 0, 1), (-1, 0, -1),
           (1, 0, -1), (-1, 0, 1), (0, 1, 1), (0, -1, -1), (0, 1, -1), (0, -1, 1)]
OPPOSITE = [0, 2, 1, 4, 3, 6, 5, 8, 7, 10, 9, 12, 11, 14, 13, 16, 15, 18, 17]
WEIGHTS = [1.0 / 3.0] + [1.0 / 18.0] * 6 + [1.0 / 36.0] * 12


def moments(stacked):
    density = stacked[0]
    for number in range(1, 19):
        density = density + stacked[number]
    velocity = []
    for direction in range(3):
        total = jnp.zeros_like(density)
        for number in range(19):
            component = LATTICE[number][direction]
            if component == 1:
                total = total + stacked[number]
            elif component == -1:
                total = total - stacked[number]
        velocity.append(total / density)
    return density, velocity


def collide(populations, solid, rate):
    density, velocity = moments(populations)
    speed = velocity[0] * velocity[0] + velocity[1] * velocity[1] + velocity[2] * velocity[2]
    collided = []
    for number in range(19):
        projection = jnp.zeros_like(density)
        for direction in range(3):
            component = LATTICE[number][direction]
            if component == 1:
                projection = projection + velocity[direction]
            elif component == -1:
                projection = projection - velocity[direction]
        equilibrium = WEIGHTS[number] * density * (1.0 + 3.0 * projection + 4.5 * projection * projection - 1.5 * speed)
        relaxed = populations[number] - rate * (populations[number] - equilibrium)
        collided.append(jnp.where(solid == 1, populations[OPPOSITE[number]], relaxed))
    return collided


def central(field, axis):
    return (-jnp.roll(field, -2, axis) + 8.0 * jnp.roll(field, -1, axis)
            - 8.0 * jnp.roll(field, 1, axis) + jnp.roll(field, 2, axis)) / 12.0


def crossing(here, there):
    return jnp.maximum(-here * there, 0.0) / (here * here + there * there + 0.25)


def reference(populations, solid, visible, omega, iso_levels, iso_index):
    collided = collide(populations, solid, omega[0])
    read = [jnp.roll(collided[number], LATTICE[number], axis=(0, 1, 2)) for number in range(19)]
    new_populations = jnp.stack(read)
    flow_density, flow = moments(read)
    grads = [[central(flow[first], second) for second in range(3)] for first in range(3)]
    inner = grads[0][0] * grads[0][0] + grads[1][1] * grads[1][1] + grads[2][2] * grads[2][2]
    inner = inner + 2.0 * (grads[0][1] * grads[1][0] + grads[0][2] * grads[2][0] + grads[1][2] * grads[2][1])
    scaled = -50.0 * inner
    choose = iso_index[:, :, None] == jnp.arange(LEVELS, dtype=jnp.int32)[None, None, :]
    brick_levels = jnp.sum(jnp.where(choose, iso_levels[None, None, :], 0.0), axis=2)
    level = jnp.repeat(jnp.repeat(brick_levels, BRICK, axis=0), BRICK, axis=1)[:, :, None]
    here = scaled - level
    cells = jnp.repeat(jnp.repeat(jnp.repeat(visible, BRICK, axis=0), BRICK, axis=1), BRICK, axis=2)
    shown = cells == 1
    weights = [jnp.where(shown, crossing(here, jnp.roll(scaled, -1, axis) - level), 0.0) for axis in range(3)]
    q_field = jnp.where(shown, scaled, 0.0)
    return new_populations, q_field, jnp.stack(weights)
```

```python
import jax
import jax.numpy as jnp
from jax import lax
from jax.experimental import pallas as pl
from jax.experimental.pallas import tpu as pltpu
from jax.sharding import PartitionSpec as P

BRICK = 16
LEVELS = 8
NXL, NYL, NZL = 8, 16, 128

LATTICE = [
    (0, 0, 0),
    (1, 0, 0),
    (-1, 0, 0),
    (0, 1, 0),
    (0, -1, 0),
    (0, 0, 1),
    (0, 0, -1),
    (1, 1, 0),
    (-1, -1, 0),
    (1, -1, 0),
    (-1, 1, 0),
    (1, 0, 1),
    (-1, 0, -1),
    (1, 0, -1),
    (-1, 0, 1),
    (0, 1, 1),
    (0, -1, -1),
    (0, 1, -1),
    (0, -1, 1),
]
UPWARD = (3, 7, 10, 15, 17)
DOWNWARD = (4, 8, 9, 16, 18)
RIGHTWARD = (1, 7, 9, 11, 13)
LEFTWARD = (2, 8, 10, 12, 14)

Y_MOMENTS = 40
UP_ROWS = (14, 15)
DOWN_ROWS = (0, 1, 2)
Y_LEN = 160
X_LEN = 280
HALO_ROWS = (-2, -1, 16, 17, 18)
PITCH = 32


def edge_start(rows):
    return Y_MOMENTS + 32 * len(rows)


def add(total, value, sign=1):
    if total is None:
        return value if sign == 1 else -value
    return total + value if sign == 1 else total - value


def row_moments(passed, row):
    dens, along_y, along_z = {}, {}, {}
    for number, (cx, cy, cz) in enumerate(LATTICE):
        source = row - cy
        if 0 <= source < NYL:
            tile = passed[number, pl.ds(source, NXL, stride=NYL), :]
            dens[cx] = add(dens.get(cx), tile)
            if cy:
                along_y[cx] = add(along_y.get(cx), tile, cy)
            if cz:
                along_z[cx] = add(along_z.get(cx), tile, cz)
    layer = lax.broadcasted_iota(jnp.int32, (NXL, NZL), 0)
    zero = jnp.zeros((NXL, NZL), jnp.float32)

    def right(tile):
        return zero if tile is None else jnp.where(layer == 0, 0.0, pltpu.roll(tile, 1, 0))

    def left(tile):
        return zero if tile is None else jnp.where(layer == NXL - 1, 0.0, pltpu.roll(tile, NXL - 1, 0))

    def joined(parts):
        return (zero if parts.get(0) is None else parts[0]) + right(parts.get(1)) + left(parts.get(-1))

    tiles = (joined(dens), right(dens.get(1)) - left(dens.get(-1)), joined(along_y), joined(along_z))

    def line(tile, which):
        return jnp.zeros((1, NZL), jnp.float32) if tile is None else tile[which : which + 1]

    beyond = [line(part.get(1), NXL - 1) for part in (dens, along_y, along_z)]
    before = [line(part.get(-1), 0) for part in (dens, along_y, along_z)]
    return tiles, beyond, before


def pack_y(passed, message, numbers, border, rows):
    for place, number in enumerate(numbers):
        message[8 * place : 8 * place + 8, :] = passed[number, pl.ds(border, NXL, stride=NYL), :]
    edge = edge_start(rows)
    for place, row in enumerate(rows):
        tiles, beyond, before = row_moments(passed, row)
        for which in range(4):
            at = Y_MOMENTS + 32 * place + 8 * which
            message[at : at + 8, :] = tiles[which]
        for which in range(3):
            at = edge + 6 * place + which
            message[at : at + 1, :] = beyond[which]
            message[at + 3 : at + 4, :] = before[which]


PAIRS = ((1, (1, 0, 0)), (3, (0, 1, 0)), (5, (0, 0, 1)), (7, (1, 1, 0)), (9, (1, -1, 0)), (11, (1, 0, 1)), (13, (1, 0, -1)), (15, (0, 1, 1)), (17, (0, 1, -1)))


def combine(parts, direction):
    total = None
    for part, sign in zip(parts, direction):
        if sign:
            total = add(total, part, sign)
    return total


def collide_kernel(omega_ref, pop, solid, passed, even_message, odd_message):
    rate = omega_ref[0]
    keep = 1.0 - rate

    def layer(i, carry):
        rows = pl.ds(pl.multiple_of(i * NYL, NYL), NYL)
        own = [pop[number, rows, :] for number in range(19)]
        wall = solid[rows, :] == 1
        differ = {number: own[number] - own[number + 1] for number, _ in PAIRS}
        density = own[0]
        for number, _ in PAIRS:
            density = density + (own[number] + own[number + 1])
        momentum = []
        for axis in range(3):
            total = None
            for number, direction in PAIRS:
                if direction[axis]:
                    total = add(total, differ[number], direction[axis])
            momentum.append(total)
        inverse = 1.0 / density
        velocity = [part * inverse for part in momentum]
        base = 1.0 - 1.5 * (velocity[0] * velocity[0] + velocity[1] * velocity[1] + velocity[2] * velocity[2])
        scale = rate * density
        weight1, weight2 = scale * (1.0 / 18.0), scale * (1.0 / 36.0)
        passed[0, rows, :] = jnp.where(wall, own[0], keep * own[0] + scale * (1.0 / 3.0) * base)
        for number, direction in PAIRS:
            along = combine(velocity, direction)
            weight = weight1 if number < 7 else weight2
            even = base + 4.5 * (along * along)
            odd = 3.0 * along
            plus = jnp.where(wall, own[number + 1], keep * own[number] + weight * (even + odd))
            minus = jnp.where(wall, own[number], keep * own[number + 1] + weight * (even - odd))
            if direction[2]:
                plus = pltpu.roll(plus, direction[2] % NZL, 1)
                minus = pltpu.roll(minus, -direction[2] % NZL, 1)
            passed[number, rows, :] = plus
            passed[number + 1, rows, :] = minus
        return carry

    lax.fori_loop(0, NXL, layer, 0)
    odd_place = lax.axis_index("gy") % 2 == 1

    @pl.when(odd_place)
    def _():
        pack_y(passed, odd_message, UPWARD, NYL - 1, UP_ROWS)
        pack_y(passed, even_message, DOWNWARD, 0, DOWN_ROWS)

    @pl.when(jnp.logical_not(odd_place))
    def _():
        pack_y(passed, even_message, UPWARD, NYL - 1, UP_ROWS)
        pack_y(passed, odd_message, DOWNWARD, 0, DOWN_ROWS)


def chooser(axis, even_message, odd_message):
    odd_place = lax.axis_index(axis) % 2 == 1

    def before(rows):
        return jnp.where(odd_place, even_message[rows, :], odd_message[rows, :])

    def after(rows):
        return jnp.where(odd_place, odd_message[rows, :], even_message[rows, :])

    return before, after


def shifted(tile, fill, step):
    row = lax.broadcasted_iota(jnp.int32, (NYL, NZL), 0)
    if step == 1:
        return jnp.where(row == 0, fill, pltpu.roll(tile, 1, 0))
    return jnp.where(row == NYL - 1, fill, pltpu.roll(tile, NYL - 1, 0))


def padded_at(layer, row):
    return (layer + 1) * PITCH + 8 + row


def moment_kernel(passed, even_in, odd_in, moments, even_out, odd_out):
    before, after = chooser("gy", even_in, odd_in)
    low = {number: before(slice(8 * place, 8 * place + 8)) for place, number in enumerate(UPWARD)}
    high = {number: after(slice(8 * place, 8 * place + 8)) for place, number in enumerate(DOWNWARD)}

    def source(number, layer):
        return passed[number, layer * NYL : (layer + 1) * NYL, :]

    def entering(numbers, signs, layer):
        step = LATTICE[numbers[0]][1]
        lines = low if step == 1 else high
        tile = fill = None
        for number, sign in zip(numbers, signs):
            tile = add(tile, source(number, layer), sign)
            fill = add(fill, lines[number][layer : layer + 1], sign)
        return shifted(tile, fill, step)

    crossing = {}
    sums = {}
    for layer in range(NXL):
        up = entering((3, 15, 17), (1, 1, 1), layer)
        down = entering((4, 16, 18), (1, 1, 1), layer)
        up_z = entering((15, 17), (1, -1), layer)
        down_z = entering((18, 16), (1, -1), layer)
        here5, here6 = source(5, layer), source(6, layer)
        sums[0, layer] = (source(0, layer) + here5 + here6 + up + down, up - down, here5 - here6 + up_z + down_z)
        for side, straight, plus, minus, rise, fall in ((1, 1, 7, 9, 11, 13), (-1, 2, 10, 8, 14, 12)):
            moved_up = entering((plus,), (1,), layer)
            moved_down = entering((minus,), (1,), layer)
            a, b = source(rise, layer), source(fall, layer)
            sums[side, layer] = (source(straight, layer) + a + b + moved_up + moved_down, moved_up - moved_down, a - b)
            if (side, layer) in ((1, NXL - 1), (-1, 0)):
                crossing[plus], crossing[minus] = moved_up, moved_down
    whole = {}
    for layer in range(NXL):
        parts = list(sums[0, layer])
        along_x = None
        if layer > 0:
            parts = [p + q for p, q in zip(parts, sums[1, layer - 1])]
            along_x = sums[1, layer - 1][0]
        if layer < NXL - 1:
            parts = [p + q for p, q in zip(parts, sums[-1, layer + 1])]
            along_x = add(along_x, sums[-1, layer + 1][0], -1)
        whole[layer] = (parts[0], along_x, parts[1], parts[2])
        for which in range(4):
            at = padded_at(layer, 0)
            moments[which, at : at + NYL, :] = whole[layer][which]
    for layer, side in ((-1, -1), (NXL, 1)):
        dens, along_y, along_z = sums[side, 0 if side == -1 else NXL - 1]
        at = padded_at(layer, 0)
        for which, value in enumerate((dens, dens if side == 1 else -dens, along_y, along_z)):
            moments[which, at : at + NYL, :] = value

    def line_of(reader, at):
        return reader(slice(at, at + 1))

    edges = {}
    for row in HALO_ROWS:
        reader, rows, place = (before, UP_ROWS, row + 2) if row < 0 else (after, DOWN_ROWS, row - 16)
        at = Y_MOMENTS + 32 * place
        tiles = [reader(slice(at + 8 * which, at + 8 * which + 8)) for which in range(4)]
        at = edge_start(rows) + 6 * place
        beyond = [line_of(reader, at + which) for which in range(3)]
        ahead = [line_of(reader, at + 3 + which) for which in range(3)]
        if row in (-1, 16):
            own_tiles, own_beyond, own_ahead = row_moments(passed, row)
            tiles = [p + q for p, q in zip(tiles, own_tiles)]
            beyond = [p + q for p, q in zip(beyond, own_beyond)]
            ahead = [p + q for p, q in zip(ahead, own_ahead)]
        for which in range(4):
            moments[which, pl.ds(padded_at(0, row), NXL, stride=PITCH), :] = tiles[which]
        for layer, lines, sign in ((-1, ahead, -1), (NXL, beyond, 1)):
            at = padded_at(layer, row)
            for which, value in enumerate((lines[0], lines[0] if sign == 1 else -lines[0], lines[1], lines[2])):
                moments[which, at : at + 1, :] = value
        edges[row] = (tiles, beyond, ahead)

    def flow_of(parts):
        inverse = 1.0 / parts[0]
        return [part * inverse for part in parts[1:]]

    def put(message, at, values):
        for value in values:
            message[at : at + value.shape[0], :] = value
            at += value.shape[0]

    def line(tiles, layer):
        return [tile[layer : layer + 1] for tile in tiles]

    def pack_right(message):
        last = NXL - 1
        put(message, 0, flow_of(whole[last - 1]))
        put(message, 48, whole[last])
        put(message, 112, [crossing[n] if n in (7, 9) else source(n, last) for n in RIGHTWARD])
        put(message, 192, flow_of(line(edges[16][0], last - 1)) + line(edges[16][0], last) + [v for row in HALO_ROWS for v in edges[row][1]])

    def pack_left(message):
        put(message, 0, whole[0])
        put(message, 64, flow_of(whole[1]) + flow_of(whole[2]))
        put(message, 160, [crossing[n] if n in (8, 10) else source(n, 0) for n in LEFTWARD])
        put(message, 240, [v for row in HALO_ROWS[:4] for v in line(edges[row][0], 0)] + flow_of(line(edges[16][0], 1)) + [v for row in HALO_ROWS for v in edges[row][2]])

    odd_place = lax.axis_index("gx") % 2 == 1

    @pl.when(odd_place)
    def _():
        pack_left(even_out)
        pack_right(odd_out)

    @pl.when(jnp.logical_not(odd_place))
    def _():
        pack_right(even_out)
        pack_left(odd_out)


def passing_kernel(passed, even_in, odd_in, new):
    before, after = chooser("gy", even_in, odd_in)
    low = {number: before(slice(8 * place, 8 * place + 8)) for place, number in enumerate(UPWARD)}
    high = {number: after(slice(8 * place, 8 * place + 8)) for place, number in enumerate(DOWNWARD)}
    for number, (cx, cy, _) in enumerate(LATTICE):
        for layer in range(NXL):
            source = layer - cx
            if not 0 <= source < NXL:
                continue
            tile = passed[number, source * NYL : (source + 1) * NYL, :]
            if cy:
                lines = low if cy == 1 else high
                tile = shifted(tile, lines[number][source : source + 1], cy)
            new[number, layer * NYL : (layer + 1) * NYL, :] = tile


def flow_at(layer, row):
    return (layer + 2) * PITCH + 8 + row


def result_kernel(visible, levels, index, moments, even_in, odd_in, new_in, new, q_field, crossings, flow, sem):
    gx, gy = lax.axis_index("gx"), lax.axis_index("gy")
    odd_place = gx % 2 == 1

    def copies(message, start, numbers, layer):
        return [
            pltpu.make_async_copy(
                message.at[start + NYL * place : start + NYL * (place + 1), :],
                new.at[number, layer * NYL : (layer + 1) * NYL, :],
                sem.at[place],
            )
            for place, number in enumerate(numbers)
        ]

    def from_left(message):
        return copies(message, 112, RIGHTWARD, 0)

    def from_right(message):
        return copies(message, 160, LEFTWARD, NXL - 1)

    def run(left_message, right_message):
        first = from_left(left_message)
        for copy in first:
            copy.start()
        compute(left_message, right_message)
        for copy in first:
            copy.wait()
        second = from_right(right_message)
        for copy in second:
            copy.start()
        for copy in second:
            copy.wait()

    def compute(left_message, right_message):
        def store_flow(layer, row, parts):
            inverse = 1.0 / parts[0]
            at = flow_at(layer, row)
            for axis in range(3):
                flow[axis, at : at + parts[0].shape[0], :] = parts[axis + 1] * inverse

        def own(layer, row, size):
            at = padded_at(layer, row)
            return [moments[which, at : at + size, :] for which in range(4)]

        def both(first, second):
            return [p + q for p, q in zip(first, second)]

        def get(message, at, count, size):
            return [message[at + size * n : at + size * (n + 1), :] for n in range(count)]

        def signed(lines, sign):
            return [lines[0], lines[0] if sign == 1 else -lines[0], lines[1], lines[2]]

        for axis, value in enumerate(get(left_message, 0, 3, NYL)):
            flow[axis, flow_at(-2, 0) : flow_at(-2, NYL), :] = value
        for axis, value in enumerate(get(left_message, 192, 3, 1)):
            flow[axis, flow_at(-2, NYL) : flow_at(-2, NYL) + 1, :] = value
        store_flow(-1, 0, both(get(left_message, 48, 4, NYL), own(-1, 0, NYL)))
        store_flow(-1, NYL, both(get(left_message, 195, 4, 1), own(-1, NYL, 1)))
        n1, n7, n9, n11, n13 = get(left_message, 112, 5, NYL)
        store_flow(0, 0, both(signed([n1 + n7 + n9 + n11 + n13, n7 - n9, n11 - n13], 1), own(0, 0, NYL)))
        for place, row in enumerate(HALO_ROWS):
            store_flow(0, row, both(signed(get(left_message, 199 + 3 * place, 3, 1), 1), own(0, row, 1)))
        for layer in range(1, NXL - 1):
            store_flow(layer, -8, own(layer, -8, PITCH))
        n2, n8, n10, n12, n14 = get(right_message, 160, 5, NYL)
        store_flow(NXL - 1, 0, both(signed([n2 + n8 + n10 + n12 + n14, n10 - n8, n14 - n12], -1), own(NXL - 1, 0, NYL)))
        for place, row in enumerate(HALO_ROWS):
            store_flow(NXL - 1, row, both(signed(get(right_message, 259 + 3 * place, 3, 1), -1), own(NXL - 1, row, 1)))
        store_flow(NXL, 0, both(get(right_message, 0, 4, NYL), own(NXL, 0, NYL)))
        for place, row in enumerate(HALO_ROWS[:4]):
            store_flow(NXL, row, both(get(right_message, 240 + 4 * place, 4, 1), own(NXL, row, 1)))
        for axis, value in enumerate(get(right_message, 64, 3, NYL)):
            flow[axis, flow_at(NXL + 1, 0) : flow_at(NXL + 1, NYL), :] = value
        for axis, value in enumerate(get(right_message, 256, 3, 1)):
            flow[axis, flow_at(NXL + 1, NYL) : flow_at(NXL + 1, NYL) + 1, :] = value
        for axis, value in enumerate(get(right_message, 112, 3, NYL)):
            flow[axis, flow_at(NXL + 2, 0) : flow_at(NXL + 2, NYL), :] = value

        def stencil(minus2, minus1, plus1, plus2):
            return 8.0 * (plus1 - minus1) + (minus2 - plus2)

        def scaled_at(load):
            grads = []
            for axis in range(3):
                centre = load(axis, 0, 0)
                grads.append(
                    (
                        stencil(*[load(axis, d, 0) for d in (-2, -1, 1, 2)]),
                        stencil(*[load(axis, 0, d) for d in (-2, -1, 1, 2)]),
                        stencil(*[pltpu.roll(centre, -d % NZL, 1) for d in (-2, -1, 1, 2)]),
                    )
                )
            inner = grads[0][0] * grads[0][0] + grads[1][1] * grads[1][1] + grads[2][2] * grads[2][2]
            inner = inner + 2.0 * (grads[0][1] * grads[1][0] + grads[0][2] * grads[2][0] + grads[1][2] * grads[2][1])
            return inner * (-50.0 / 144.0)

        def layer_load(layer):
            def load(axis, dx, dy):
                at = flow_at(layer + dx, dy)
                return flow[axis, at : at + NYL, :]

            return load

        def row_load(axis, dx, dy):
            return flow[axis, pl.ds(flow_at(dx, NYL + dy), NXL, stride=PITCH), :]

        level = levels[index[gx * NXL // BRICK, gy * NYL // BRICK]]
        lane = lax.broadcasted_iota(jnp.int32, (NYL, NZL), 1) // BRICK
        shown = jnp.zeros((NYL, NZL), jnp.int32)
        for brick in range(NZL // BRICK):
            shown = jnp.where(lane == brick, visible[gx * NXL // BRICK, gy * NYL // BRICK, brick], shown)
        shown = shown == 1

        def crossing(here, there):
            return jnp.where(shown, jnp.maximum(-here * there, 0.0) / (here * here + there * there + 0.25), 0.0)

        above = scaled_at(row_load)
        following = scaled_at(layer_load(0))
        for layer in range(NXL):
            scaled, following = following, scaled_at(layer_load(layer + 1))
            at = layer * NYL
            here = scaled - level
            q_field[at : at + NYL, :] = jnp.where(shown, scaled, 0.0)
            crossings[0, at : at + NYL, :] = crossing(here, following - level)
            crossings[1, at : at + NYL, :] = crossing(here, shifted(scaled, above[layer : layer + 1], -1) - level)
            crossings[2, at : at + NYL, :] = crossing(here, pltpu.roll(here, NZL - 1, 1))

    @pl.when(odd_place)
    def _():
        run(even_in, odd_in)

    @pl.when(jnp.logical_not(odd_place))
    def _():
        run(odd_in, even_in)


def swap(value, axis, parity):
    size = lax.axis_size(axis)
    pairs = []
    for i in range(size):
        mate = i + 1 if i % 2 == parity else i - 1
        pairs.append((i, mate % size))
    return lax.ppermute(value, axis, pairs)


VMEM = pl.BlockSpec(memory_space=pltpu.VMEM)
SMEM = pl.BlockSpec(memory_space=pltpu.SMEM)
ANY = pl.BlockSpec(memory_space=pl.ANY)


def shape(*dims):
    return jax.ShapeDtypeStruct(dims, jnp.float32)


def per_device(populations, solid, visible, omega, iso_levels, iso_index):
    cells = NXL * NYL
    passed, to_even, to_odd = pl.pallas_call(
        collide_kernel,
        out_shape=(shape(19, cells, NZL), shape(Y_LEN, NZL), shape(Y_LEN, NZL)),
        in_specs=[SMEM, VMEM, VMEM],
        out_specs=(VMEM, VMEM, VMEM),
    )(omega, populations.reshape(19, cells, NZL), solid.reshape(cells, NZL))
    odd_y = swap(to_odd, "gy", 1)
    even_y = swap(to_even, "gy", 0)
    moments, to_even, to_odd = pl.pallas_call(
        moment_kernel,
        out_shape=(shape(4, (NXL + 2) * PITCH, NZL), shape(X_LEN, NZL), shape(X_LEN, NZL)),
        in_specs=[VMEM, VMEM, VMEM],
        out_specs=(VMEM, VMEM, VMEM),
    )(passed, even_y, odd_y)
    odd_x = swap(to_odd, "gx", 1)
    even_x = swap(to_even, "gx", 0)
    new = pl.pallas_call(
        passing_kernel,
        out_shape=shape(19, cells, NZL),
        in_specs=[VMEM, VMEM, VMEM],
        out_specs=VMEM,
    )(passed, even_y, odd_y)
    new, q_field, crossings = pl.pallas_call(
        result_kernel,
        out_shape=(shape(19, cells, NZL), shape(cells, NZL), shape(3, cells, NZL)),
        in_specs=[SMEM, SMEM, SMEM, VMEM, VMEM, VMEM, ANY],
        out_specs=(ANY, VMEM, VMEM),
        scratch_shapes=[pltpu.VMEM((3, (NXL + 5) * PITCH, NZL), jnp.float32), pltpu.SemaphoreType.DMA((5,))],
        input_output_aliases={6: 0},
    )(visible, iso_levels, iso_index, moments, even_x, odd_x, new)
    return (
        new.reshape(19, NXL, NYL, NZL),
        q_field.reshape(NXL, NYL, NZL),
        crossings.reshape(3, NXL, NYL, NZL),
    )


def solution(mesh):
    in_specs = (P(None, "gx", "gy", None), P("gx", "gy", None), P(), P(), P(), P())
    out_specs = (P(None, "gx", "gy", None), P("gx", "gy", None), P(None, "gx", "gy", None))
    return jax.shard_map(
        per_device, mesh=mesh, in_specs=in_specs, out_specs=out_specs, check_vma=False
    )
```

```python
import jax
import jax.numpy as jnp
from jax import lax
from jax.experimental import pallas as pl
from jax.experimental.pallas import tpu as pltpu
from jax.sharding import PartitionSpec as P

BRICK = 16
LEVELS = 8
NXL, NYL, NZL = 8, 16, 128

LATTICE = [
    (0, 0, 0),
    (1, 0, 0),
    (-1, 0, 0),
    (0, 1, 0),
    (0, -1, 0),
    (0, 0, 1),
    (0, 0, -1),
    (1, 1, 0),
    (-1, -1, 0),
    (1, -1, 0),
    (-1, 1, 0),
    (1, 0, 1),
    (-1, 0, -1),
    (1, 0, -1),
    (-1, 0, 1),
    (0, 1, 1),
    (0, -1, -1),
    (0, 1, -1),
    (0, -1, 1),
]
UPWARD = (3, 7, 10, 15, 17)
DOWNWARD = (4, 8, 9, 16, 18)
RIGHTWARD = (1, 7, 9, 11, 13)
LEFTWARD = (2, 8, 10, 12, 14)

Y_MOMENTS = 40
UP_ROWS = (14, 15)
DOWN_ROWS = (0, 1, 2)
Y_LEN = 160
X_LEN = 280
HALO_ROWS = (-2, -1, 16, 17, 18)
PITCH = 32


def edge_start(rows):
    return Y_MOMENTS + 32 * len(rows)


def add(total, value, sign=1):
    if total is None:
        return value if sign == 1 else -value
    return total + value if sign == 1 else total - value


def row_moments(passed, row):
    return tile_moments(
        {
            number: passed[number, pl.ds(row - cy, NXL, stride=NYL), :]
            for number, (_, cy, _) in enumerate(LATTICE)
            if 0 <= row - cy < NYL
        }
    )


def tile_moments(tiles):
    dens, along_y, along_z = {}, {}, {}
    for number, (cx, cy, cz) in enumerate(LATTICE):
        if number in tiles:
            tile = tiles[number]
            dens[cx] = add(dens.get(cx), tile)
            if cy:
                along_y[cx] = add(along_y.get(cx), tile, cy)
            if cz:
                along_z[cx] = add(along_z.get(cx), tile, cz)
    layer = lax.broadcasted_iota(jnp.int32, (NXL, NZL), 0)
    zero = jnp.zeros((NXL, NZL), jnp.float32)

    def right(tile):
        return zero if tile is None else jnp.where(layer == 0, 0.0, pltpu.roll(tile, 1, 0))

    def left(tile):
        return zero if tile is None else jnp.where(layer == NXL - 1, 0.0, pltpu.roll(tile, NXL - 1, 0))

    def joined(parts):
        return (zero if parts.get(0) is None else parts[0]) + right(parts.get(1)) + left(parts.get(-1))

    tiles = (joined(dens), right(dens.get(1)) - left(dens.get(-1)), joined(along_y), joined(along_z))

    def line(tile, which):
        return jnp.zeros((1, NZL), jnp.float32) if tile is None else tile[which : which + 1]

    beyond = [line(part.get(1), NXL - 1) for part in (dens, along_y, along_z)]
    before = [line(part.get(-1), 0) for part in (dens, along_y, along_z)]
    return tiles, beyond, before


def pack_y(passed, message, numbers, border, rows):
    for place, number in enumerate(numbers):
        message[8 * place : 8 * place + 8, :] = passed[number, pl.ds(border, NXL, stride=NYL), :]
    edge = edge_start(rows)
    for place, row in enumerate(rows):
        tiles, beyond, before = row_moments(passed, row)
        for which in range(4):
            at = Y_MOMENTS + 32 * place + 8 * which
            message[at : at + 8, :] = tiles[which]
        for which in range(3):
            at = edge + 6 * place + which
            message[at : at + 1, :] = beyond[which]
            message[at + 3 : at + 4, :] = before[which]


PAIRS = ((1, (1, 0, 0)), (3, (0, 1, 0)), (5, (0, 0, 1)), (7, (1, 1, 0)), (9, (1, -1, 0)), (11, (1, 0, 1)), (13, (1, 0, -1)), (15, (0, 1, 1)), (17, (0, 1, -1)))


def combine(parts, direction):
    total = None
    for part, sign in zip(parts, direction):
        if sign:
            total = add(total, part, sign)
    return total


def collide_kernel(omega_ref, pop_in, solid_in, passed, odd_message, even_message, pop, solid, sem):
    rate = omega_ref[0]
    keep = 1.0 - rate

    def loads(i):
        rows = pl.ds(pl.multiple_of(i * NYL, NYL), NYL)
        return (
            pltpu.make_async_copy(pop_in.at[:, rows, :], pop.at[:, rows, :], sem.at[0, i]),
            pltpu.make_async_copy(solid_in.at[rows, :], solid.at[rows, :], sem.at[1, i]),
        )

    for i in range(NXL):
        for copy in loads(i):
            copy.start()

    def layer(i, carry):
        for copy in loads(i):
            copy.wait()
        rows = pl.ds(pl.multiple_of(i * NYL, NYL), NYL)
        own = [pop[number, rows, :] for number in range(19)]
        wall = solid[rows, :] == 1
        differ = {number: own[number] - own[number + 1] for number, _ in PAIRS}
        density = own[0]
        for number, _ in PAIRS:
            density = density + (own[number] + own[number + 1])
        momentum = [combine([differ[number] for number, _ in PAIRS], [d[axis] for _, d in PAIRS]) for axis in range(3)]
        inverse = 1.0 / density
        velocity = [part * inverse for part in momentum]
        base = 1.0 - 1.5 * (velocity[0] * velocity[0] + velocity[1] * velocity[1] + velocity[2] * velocity[2])
        scale = rate * density
        weight1, weight2 = scale * (1.0 / 18.0), scale * (1.0 / 36.0)
        passed[0, rows, :] = jnp.where(wall, own[0], keep * own[0] + scale * (1.0 / 3.0) * base)
        for number, direction in PAIRS:
            along = combine(velocity, direction)
            weight = weight1 if number < 7 else weight2
            even = base + 4.5 * (along * along)
            odd = 3.0 * along
            plus = jnp.where(wall, own[number + 1], keep * own[number] + weight * (even + odd))
            minus = jnp.where(wall, own[number], keep * own[number + 1] + weight * (even - odd))
            if direction[2]:
                plus = pltpu.roll(plus, direction[2] % NZL, 1)
                minus = pltpu.roll(minus, -direction[2] % NZL, 1)
            passed[number, rows, :] = plus
            passed[number + 1, rows, :] = minus
        return carry

    lax.fori_loop(0, NXL, layer, 0)
    odd_place = lax.axis_index("gy") % 2 == 1

    @pl.when(odd_place)
    def _():
        pack_y(passed, odd_message, UPWARD, NYL - 1, UP_ROWS)
        pack_y(passed, even_message, DOWNWARD, 0, DOWN_ROWS)

    @pl.when(jnp.logical_not(odd_place))
    def _():
        pack_y(passed, even_message, UPWARD, NYL - 1, UP_ROWS)
        pack_y(passed, odd_message, DOWNWARD, 0, DOWN_ROWS)


def chooser(axis, even_message, odd_message):
    odd_place = lax.axis_index(axis) % 2 == 1

    def before(rows):
        return jnp.where(odd_place, even_message[rows, :], odd_message[rows, :])

    def after(rows):
        return jnp.where(odd_place, odd_message[rows, :], even_message[rows, :])

    return before, after


def shifted(tile, fill, step):
    row = lax.broadcasted_iota(jnp.int32, (NYL, NZL), 0)
    if step == 1:
        return jnp.where(row == 0, fill, pltpu.roll(tile, 1, 0))
    return jnp.where(row == NYL - 1, fill, pltpu.roll(tile, NYL - 1, 0))


def padded_at(layer, row):
    return (layer + 1) * PITCH + 8 + row


def moment_kernel(passed, moments):
    def source(number, layer):
        return passed[number, layer * NYL : (layer + 1) * NYL, :]

    def entering(numbers, signs, layer):
        tile = None
        for number, sign in zip(numbers, signs):
            tile = add(tile, source(number, layer), sign)
        return shifted(tile, 0.0, LATTICE[numbers[0]][1])

    def own_sums(layer):
        up = entering((3, 15, 17), (1, 1, 1), layer)
        down = entering((4, 16, 18), (1, 1, 1), layer)
        up_z = entering((15, 17), (1, -1), layer)
        down_z = entering((18, 16), (1, -1), layer)
        here5, here6 = source(5, layer), source(6, layer)
        return (source(0, layer) + here5 + here6 + up + down, up - down, here5 - here6 + up_z + down_z)

    def side_sums(layer, straight, plus, minus, rise, fall):
        moved_up = entering((plus,), (1,), layer)
        moved_down = entering((minus,), (1,), layer)
        a, b = source(rise, layer), source(fall, layer)
        return (source(straight, layer) + a + b + moved_up + moved_down, moved_up - moved_down, a - b)

    def to_right(layer):
        return side_sums(layer, 1, 7, 9, 11, 13)

    def to_left(layer):
        return side_sums(layer, 2, 10, 8, 14, 12)

    def store(layer, values):
        at = padded_at(layer, 0)
        for which in range(4):
            moments[which, at : at + NYL, :] = values[which]

    for layer in range(NXL):
        parts, along_x = list(own_sums(layer)), None
        if layer > 0:
            extra = to_right(layer - 1)
            parts, along_x = [p + q for p, q in zip(parts, extra)], extra[0]
        if layer < NXL - 1:
            extra = to_left(layer + 1)
            parts, along_x = [p + q for p, q in zip(parts, extra)], add(along_x, extra[0], -1)
        store(layer, (parts[0], along_x, parts[1], parts[2]))
    dens, along_y, along_z = to_left(0)
    store(-1, (dens, -dens, along_y, along_z))
    dens, along_y, along_z = to_right(NXL - 1)
    store(NXL, (dens, dens, along_y, along_z))
    for row in (-1, NYL):
        tiles, beyond, ahead = row_moments(passed, row)
        store_row(moments, row, tiles, beyond, ahead)


def store_row(moments, row, tiles, beyond, ahead):
    for which in range(4):
        moments[which, pl.ds(padded_at(0, row), NXL, stride=PITCH), :] = tiles[which]
    for layer, lines, sign in ((-1, ahead, -1), (NXL, beyond, 1)):
        at = padded_at(layer, row)
        for which, value in enumerate((lines[0], lines[0] if sign == 1 else -lines[0], lines[1], lines[2])):
            moments[which, at : at + 1, :] = value


def load_row(moments, row):
    tiles = [moments[which, pl.ds(padded_at(0, row), NXL, stride=PITCH), :] for which in range(4)]
    beyond, ahead = (
        [moments[which, padded_at(layer, row) : padded_at(layer, row) + 1, :] for which in (0, 2, 3)]
        for layer in (NXL, -1)
    )
    return tiles, beyond, ahead


def joining_kernel(passed, odd_in, even_in, moments_in, moments, odd_out, even_out):
    moments[...] = moments_in[...]
    before, after = chooser("gy", even_in, odd_in)
    low = {number: before(slice(8 * place, 8 * place + 8)) for place, number in enumerate(UPWARD)}
    high = {number: after(slice(8 * place, 8 * place + 8)) for place, number in enumerate(DOWNWARD)}

    def line_of(reader, at):
        return reader(slice(at, at + 1))

    def sums(first, second):
        return [[p + q for p, q in zip(a, b)] for a, b in zip(first, second)]

    edges = {}
    for row, lines in ((0, low), (NYL - 1, high)):
        store_row(moments, row, *sums(load_row(moments, row), tile_moments(lines)))
    for row in HALO_ROWS:
        reader, rows, place = (before, UP_ROWS, row + 2) if row < 0 else (after, DOWN_ROWS, row - 16)
        at = Y_MOMENTS + 32 * place
        tiles = [reader(slice(at + 8 * which, at + 8 * which + 8)) for which in range(4)]
        at = edge_start(rows) + 6 * place
        beyond = [line_of(reader, at + which) for which in range(3)]
        ahead = [line_of(reader, at + 3 + which) for which in range(3)]
        if row in (-1, 16):
            tiles, beyond, ahead = sums(load_row(moments, row), (tiles, beyond, ahead))
        store_row(moments, row, tiles, beyond, ahead)
        edges[row] = (tiles, beyond, ahead)

    def flow_of(parts):
        inverse = 1.0 / parts[0]
        return [part * inverse for part in parts[1:]]

    def put(message, at, values):
        for value in values:
            message[at : at + value.shape[0], :] = value
            at += value.shape[0]

    def line(tiles, layer):
        return [tile[layer : layer + 1] for tile in tiles]

    def whole(layer):
        at = padded_at(layer, 0)
        return [moments[which, at : at + NYL, :] for which in range(4)]

    def leaving(number, layer):
        tile = passed[number, layer * NYL : (layer + 1) * NYL, :]
        cy = LATTICE[number][1]
        if cy:
            tile = shifted(tile, (low if cy == 1 else high)[number][layer : layer + 1], cy)
        return tile

    def pack_right(message):
        last = NXL - 1
        put(message, 0, flow_of(whole(last - 1)))
        put(message, 48, whole(last))
        put(message, 112, [leaving(number, last) for number in RIGHTWARD])
        put(message, 192, flow_of(line(edges[16][0], last - 1)) + line(edges[16][0], last) + [v for row in HALO_ROWS for v in edges[row][1]])

    def pack_left(message):
        put(message, 0, whole(0))
        put(message, 64, flow_of(whole(1)) + flow_of(whole(2)))
        put(message, 160, [leaving(number, 0) for number in LEFTWARD])
        put(message, 240, [v for row in HALO_ROWS[:4] for v in line(edges[row][0], 0)] + flow_of(line(edges[16][0], 1)) + [v for row in HALO_ROWS for v in edges[row][2]])

    odd_place = lax.axis_index("gx") % 2 == 1

    @pl.when(odd_place)
    def _():
        pack_right(odd_out)
        pack_left(even_out)

    @pl.when(jnp.logical_not(odd_place))
    def _():
        pack_left(odd_out)
        pack_right(even_out)


def passing_kernel(visible, levels, index, passed, odd_in, even_in, moments, new, flow, shades):
    before, after = chooser("gy", even_in, odd_in)
    low = {number: before(slice(8 * place, 8 * place + 8)) for place, number in enumerate(UPWARD)}
    high = {number: after(slice(8 * place, 8 * place + 8)) for place, number in enumerate(DOWNWARD)}
    for number, (cx, cy, _) in enumerate(LATTICE):
        for layer in range(NXL):
            source = layer - cx
            if not 0 <= source < NXL:
                continue
            tile = passed[number, source * NYL : (source + 1) * NYL, :]
            if cy:
                lines = low if cy == 1 else high
                tile = shifted(tile, lines[number][source : source + 1], cy)
            new[number, layer * NYL : (layer + 1) * NYL, :] = tile
    for layer in range(1, NXL - 1):
        at = padded_at(layer, -8)
        inverse = 1.0 / moments[0, at : at + PITCH, :]
        to = flow_at(layer, -8)
        for axis in range(3):
            flow[axis, to : to + PITCH, :] = moments[axis + 1, at : at + PITCH, :] * inverse
    brick_x, brick_y = lax.axis_index("gx") * NXL // BRICK, lax.axis_index("gy") * NYL // BRICK
    lane = lax.broadcasted_iota(jnp.int32, (8, NZL), 1) // BRICK
    shown = jnp.zeros((8, NZL), jnp.int32)
    for brick in range(NZL // BRICK):
        shown = jnp.where(lane == brick, visible[brick_x, brick, brick_y], shown)
    shades[0:8, :] = shown.astype(jnp.float32)
    shades[8:16, :] = jnp.full((8, NZL), levels[index[brick_x, brick_y]], jnp.float32)


def flow_at(layer, row):
    return (layer + 2) * PITCH + 8 + row


def result_kernel(shades, moments, odd_in, even_in, inner_flow, new_in, new, q_field, crossings, outer_flow, q_held, c_held, sem, out_sem):
    del new_in
    odd_place = lax.axis_index("gx") % 2 == 1

    def copies(message, start, numbers, layer, first):
        return [
            pltpu.make_async_copy(
                message.at[start + NYL * place : start + NYL * (place + 1), :],
                new.at[number, layer * NYL : (layer + 1) * NYL, :],
                sem.at[first + place],
            )
            for place, number in enumerate(numbers)
        ]

    def run(left_message, right_message):
        copied = copies(left_message, 112, RIGHTWARD, 0, 0) + copies(right_message, 160, LEFTWARD, NXL - 1, 5)
        for copy in copied:
            copy.start()
        copied += compute(left_message, right_message)
        for copy in copied:
            copy.wait()

    def stores(layer):
        rows = slice(layer * NYL, (layer + 2) * NYL)
        return [
            pltpu.make_async_copy(q_held.at[rows, :], q_field.at[rows, :], out_sem.at[0, layer // 2]),
            pltpu.make_async_copy(c_held.at[:, rows, :], crossings.at[:, rows, :], out_sem.at[1, layer // 2]),
        ]

    def flow_ref(layer):
        return inner_flow if 0 < layer < NXL - 1 else outer_flow

    def compute(left_message, right_message):
        flow = outer_flow
        started = []

        def store_flow(layer, row, parts):
            inverse = 1.0 / parts[0]
            at = flow_at(layer, row)
            for axis in range(3):
                flow[axis, at : at + parts[0].shape[0], :] = parts[axis + 1] * inverse

        def own(layer, row, size):
            at = padded_at(layer, row)
            return [moments[which, at : at + size, :] for which in range(4)]

        def both(first, second):
            return [p + q for p, q in zip(first, second)]

        def get(message, at, count, size):
            return [message[at + size * n : at + size * (n + 1), :] for n in range(count)]

        def signed(lines, sign):
            return [lines[0], lines[0] if sign == 1 else -lines[0], lines[1], lines[2]]

        for axis, value in enumerate(get(left_message, 0, 3, NYL)):
            flow[axis, flow_at(-2, 0) : flow_at(-2, NYL), :] = value
        for axis, value in enumerate(get(left_message, 192, 3, 1)):
            flow[axis, flow_at(-2, NYL) : flow_at(-2, NYL) + 1, :] = value
        store_flow(-1, 0, both(get(left_message, 48, 4, NYL), own(-1, 0, NYL)))
        store_flow(-1, NYL, both(get(left_message, 195, 4, 1), own(-1, NYL, 1)))
        n1, n7, n9, n11, n13 = get(left_message, 112, 5, NYL)
        store_flow(0, 0, both(signed([n1 + n7 + n9 + n11 + n13, n7 - n9, n11 - n13], 1), own(0, 0, NYL)))
        for place, row in enumerate(HALO_ROWS):
            store_flow(0, row, both(signed(get(left_message, 199 + 3 * place, 3, 1), 1), own(0, row, 1)))
        n2, n8, n10, n12, n14 = get(right_message, 160, 5, NYL)
        store_flow(NXL - 1, 0, both(signed([n2 + n8 + n10 + n12 + n14, n10 - n8, n14 - n12], -1), own(NXL - 1, 0, NYL)))
        for place, row in enumerate(HALO_ROWS):
            store_flow(NXL - 1, row, both(signed(get(right_message, 259 + 3 * place, 3, 1), -1), own(NXL - 1, row, 1)))
        store_flow(NXL, 0, both(get(right_message, 0, 4, NYL), own(NXL, 0, NYL)))
        for place, row in enumerate(HALO_ROWS[:4]):
            store_flow(NXL, row, both(get(right_message, 240 + 4 * place, 4, 1), own(NXL, row, 1)))
        for axis, value in enumerate(get(right_message, 64, 3, NYL)):
            flow[axis, flow_at(NXL + 1, 0) : flow_at(NXL + 1, NYL), :] = value
        for axis, value in enumerate(get(right_message, 256, 3, 1)):
            flow[axis, flow_at(NXL + 1, NYL) : flow_at(NXL + 1, NYL) + 1, :] = value
        for axis, value in enumerate(get(right_message, 112, 3, NYL)):
            flow[axis, flow_at(NXL + 2, 0) : flow_at(NXL + 2, NYL), :] = value

        def stencil(minus2, minus1, plus1, plus2):
            return 8.0 * (plus1 - minus1) + (minus2 - plus2)

        def scaled_at(load):
            grads = []
            for axis in range(3):
                centre = load(axis, 0, 0)
                grads.append(
                    (
                        stencil(*[load(axis, d, 0) for d in (-2, -1, 1, 2)]),
                        stencil(*[load(axis, 0, d) for d in (-2, -1, 1, 2)]),
                        stencil(*[pltpu.roll(centre, -d % NZL, 1) for d in (-2, -1, 1, 2)]),
                    )
                )
            inner = grads[0][0] * grads[0][0] + grads[1][1] * grads[1][1] + grads[2][2] * grads[2][2]
            inner = inner + 2.0 * (grads[0][1] * grads[1][0] + grads[0][2] * grads[2][0] + grads[1][2] * grads[2][1])
            return inner * (-50.0 / 144.0)

        def layer_load(layer):
            def load(axis, dx, dy):
                at = flow_at(layer + dx, dy)
                return flow_ref(layer + dx)[axis, at : at + NYL, :]

            return load

        lines = lax.broadcasted_iota(jnp.int32, (NXL, NZL), 0)

        def row_load(axis, dx, dy):
            rows = pl.ds(flow_at(dx, NYL + dy), NXL, stride=PITCH)
            inside = jnp.logical_and(lines + dx > 0, lines + dx < NXL - 1)
            return jnp.where(inside, inner_flow[axis, rows, :], outer_flow[axis, rows, :])

        shown = shades[0:1, :] > 0.5
        level = shades[8:9, :]

        def crossing(here, there):
            return jnp.where(shown, jnp.maximum(-here * there, 0.0) / (here * here + there * there + 0.25), 0.0)

        above = scaled_at(row_load)
        following = scaled_at(layer_load(0))
        for layer in range(NXL):
            scaled, following = following, scaled_at(layer_load(layer + 1))
            at = layer * NYL
            here = scaled - level
            q_held[at : at + NYL, :] = jnp.where(shown, scaled, 0.0)
            c_held[0, at : at + NYL, :] = crossing(here, following - level)
            c_held[1, at : at + NYL, :] = crossing(here, shifted(scaled, above[layer : layer + 1], -1) - level)
            c_held[2, at : at + NYL, :] = crossing(here, pltpu.roll(here, NZL - 1, 1))
            if layer % 2:
                for copy in stores(layer - 1):
                    copy.start()
                    started.append(copy)
        return started

    @pl.when(odd_place)
    def _():
        run(even_in, odd_in)

    @pl.when(jnp.logical_not(odd_place))
    def _():
        run(odd_in, even_in)


def swap(value, axis, parity):
    size = lax.axis_size(axis)
    pairs = []
    for i in range(size):
        mate = i + 1 if i % 2 == parity else i - 1
        pairs.append((i, mate % size))
    return lax.ppermute(value, axis, pairs)


VMEM = pl.BlockSpec(memory_space=pltpu.VMEM)
SMEM = pl.BlockSpec(memory_space=pltpu.SMEM)
ANY = pl.BlockSpec(memory_space=pl.ANY)
HBM = pl.BlockSpec(memory_space=pltpu.HBM)


def shape(*dims):
    return jax.ShapeDtypeStruct(dims, jnp.float32)


def held(*dims):
    return pltpu.VMEM(dims, jnp.float32)


LARGE = pltpu.CompilerParams(vmem_limit_bytes=61 << 20)
SMALL = pltpu.CompilerParams(vmem_limit_bytes=8 << 20)


def near(value):
    return pltpu.with_memory_space_constraint(value, pltpu.VMEM)


def per_device(populations, solid, visible, omega, iso_levels, iso_index):
    cells = NXL * NYL
    padded = (3, (NXL + 5) * PITCH, NZL)
    passed, to_odd, to_even = pl.pallas_call(
        collide_kernel,
        out_shape=(held(19, cells, NZL), held(Y_LEN, NZL), held(Y_LEN, NZL)),
        in_specs=[SMEM, HBM, HBM],
        out_specs=(VMEM, VMEM, VMEM),
        compiler_params=LARGE,
        scratch_shapes=[
            pltpu.VMEM((19, cells, NZL), jnp.float32),
            pltpu.VMEM((cells, NZL), jnp.int32),
            pltpu.SemaphoreType.DMA((2, NXL)),
        ],
    )(omega, populations.reshape(19, cells, NZL), solid.reshape(cells, NZL))
    passed = near(passed)
    odd_y = near(swap(to_odd, "gy", 1))
    even_y = near(swap(to_even, "gy", 0))
    moments = pl.pallas_call(
        moment_kernel,
        out_shape=held(4, (NXL + 2) * PITCH, NZL),
        in_specs=[VMEM],
        out_specs=VMEM,
        compiler_params=SMALL,
    )(passed)
    moments, to_odd, to_even = pl.pallas_call(
        joining_kernel,
        out_shape=(held(4, (NXL + 2) * PITCH, NZL), held(X_LEN, NZL), held(X_LEN, NZL)),
        in_specs=[VMEM, VMEM, VMEM, VMEM],
        out_specs=(VMEM, VMEM, VMEM),
        compiler_params=SMALL,
    )(passed, odd_y, even_y, near(moments))
    moments = near(moments)
    odd_x = near(swap(to_odd, "gx", 1))
    even_x = near(swap(to_even, "gx", 0))
    new, flow, shades = pl.pallas_call(
        passing_kernel,
        out_shape=(shape(19, cells, NZL), held(*padded), held(16, NZL)),
        in_specs=[SMEM, SMEM, SMEM, VMEM, VMEM, VMEM, VMEM],
        out_specs=(VMEM, VMEM, VMEM),
        compiler_params=SMALL,
    )(visible.transpose(0, 2, 1), iso_levels, iso_index, passed, odd_y, even_y, moments)
    new, q_field, crossings = pl.pallas_call(
        result_kernel,
        out_shape=(shape(19, cells, NZL), shape(cells, NZL), shape(3, cells, NZL)),
        in_specs=[VMEM, VMEM, VMEM, VMEM, VMEM, ANY],
        out_specs=(ANY, ANY, ANY),
        compiler_params=SMALL,
        scratch_shapes=[
            pltpu.VMEM(padded, jnp.float32),
            pltpu.VMEM((cells, NZL), jnp.float32),
            pltpu.VMEM((3, cells, NZL), jnp.float32),
            pltpu.SemaphoreType.DMA((10,)),
            pltpu.SemaphoreType.DMA((2, NXL // 2)),
        ],
        input_output_aliases={5: 0},
    )(near(shades), moments, odd_x, even_x, near(flow), new)
    return (
        new.reshape(19, NXL, NYL, NZL),
        q_field.reshape(NXL, NYL, NZL),
        crossings.reshape(3, NXL, NYL, NZL),
    )


def solution(mesh):
    in_specs = (P(None, "gx", "gy", None), P("gx", "gy", None), P(), P(), P(), P())
    out_specs = (P(None, "gx", "gy", None), P("gx", "gy", None), P(None, "gx", "gy", None))
    return jax.shard_map(
        per_device, mesh=mesh, in_specs=in_specs, out_specs=out_specs, check_vma=False
    )
```

```python
import jax
import jax.numpy as jnp
from jax import lax
from jax.experimental import pallas as pl
from jax.experimental.pallas import tpu as pltpu
from jax.sharding import PartitionSpec as P

BRICK = 16
LEVELS = 8
NXL, NYL, NZL = 8, 16, 128

LATTICE = [
    (0, 0, 0),
    (1, 0, 0),
    (-1, 0, 0),
    (0, 1, 0),
    (0, -1, 0),
    (0, 0, 1),
    (0, 0, -1),
    (1, 1, 0),
    (-1, -1, 0),
    (1, -1, 0),
    (-1, 1, 0),
    (1, 0, 1),
    (-1, 0, -1),
    (1, 0, -1),
    (-1, 0, 1),
    (0, 1, 1),
    (0, -1, -1),
    (0, 1, -1),
    (0, -1, 1),
]
UPWARD = (3, 7, 10, 15, 17)
DOWNWARD = (4, 8, 9, 16, 18)
RIGHTWARD = (1, 7, 9, 11, 13)
LEFTWARD = (2, 8, 10, 12, 14)

Y_MOMENTS = 40
UP_ROWS = (14, 15)
DOWN_ROWS = (0, 1, 2)
Y_LEN = 160
X_LEN = 280
HALO_ROWS = (-2, -1, 16, 17, 18)
PITCH = 32


def edge_start(rows):
    return Y_MOMENTS + 32 * len(rows)


def add(total, value, sign=1):
    if total is None:
        return value if sign == 1 else -value
    return total + value if sign == 1 else total - value


def row_moments(load, row):
    return tile_moments(
        {number: load(number, row - cy) for number, (_, cy, _) in enumerate(LATTICE) if 0 <= row - cy < NYL}
    )


def tile_moments(tiles):
    dens, along_y, along_z = {}, {}, {}
    for number, (cx, cy, cz) in enumerate(LATTICE):
        if number in tiles:
            tile = tiles[number]
            dens[cx] = add(dens.get(cx), tile)
            if cy:
                along_y[cx] = add(along_y.get(cx), tile, cy)
            if cz:
                along_z[cx] = add(along_z.get(cx), tile, cz)
    layer = lax.broadcasted_iota(jnp.int32, (NXL, NZL), 0)
    zero = jnp.zeros((NXL, NZL), jnp.float32)

    def right(tile):
        return zero if tile is None else jnp.where(layer == 0, 0.0, pltpu.roll(tile, 1, 0))

    def left(tile):
        return zero if tile is None else jnp.where(layer == NXL - 1, 0.0, pltpu.roll(tile, NXL - 1, 0))

    def joined(parts):
        return (zero if parts.get(0) is None else parts[0]) + right(parts.get(1)) + left(parts.get(-1))

    tiles = (joined(dens), right(dens.get(1)) - left(dens.get(-1)), joined(along_y), joined(along_z))

    def line(tile, which):
        return jnp.zeros((1, NZL), jnp.float32) if tile is None else tile[which : which + 1]

    beyond = [line(part.get(1), NXL - 1) for part in (dens, along_y, along_z)]
    before = [line(part.get(-1), 0) for part in (dens, along_y, along_z)]
    return tiles, beyond, before


def pack_y(load, message, numbers, border, rows):
    for place, number in enumerate(numbers):
        message[8 * place : 8 * place + 8, :] = load(number, border)
    edge = edge_start(rows)
    for place, row in enumerate(rows):
        tiles, beyond, before = row_moments(load, row)
        for which in range(4):
            at = Y_MOMENTS + 32 * place + 8 * which
            message[at : at + 8, :] = tiles[which]
        for which in range(3):
            at = edge + 6 * place + which
            message[at : at + 1, :] = beyond[which]
            message[at + 3 : at + 4, :] = before[which]


PAIRS = ((1, (1, 0, 0)), (3, (0, 1, 0)), (5, (0, 0, 1)), (7, (1, 1, 0)), (9, (1, -1, 0)), (11, (1, 0, 1)), (13, (1, 0, -1)), (15, (0, 1, 1)), (17, (0, 1, -1)))


def combine(parts, direction):
    total = None
    for part, sign in zip(parts, direction):
        if sign:
            total = add(total, part, sign)
    return total


def collided(own, wall, rate):
    keep = 1.0 - rate
    differ = {number: own[number] - own[number + 1] for number, _ in PAIRS}
    density = own[0]
    for number, _ in PAIRS:
        density = density + (own[number] + own[number + 1])
    momentum = [combine([differ[number] for number, _ in PAIRS], [d[axis] for _, d in PAIRS]) for axis in range(3)]
    inverse = 1.0 / density
    velocity = [part * inverse for part in momentum]
    base = 1.0 - 1.5 * (velocity[0] * velocity[0] + velocity[1] * velocity[1] + velocity[2] * velocity[2])
    scale = rate * density
    weight1, weight2 = scale * (1.0 / 18.0), scale * (1.0 / 36.0)
    yield 0, jnp.where(wall, own[0], keep * own[0] + scale * (1.0 / 3.0) * base)
    for number, direction in PAIRS:
        along = combine(velocity, direction)
        weight = weight1 if number < 7 else weight2
        even = base + 4.5 * (along * along)
        odd = 3.0 * along
        plus = jnp.where(wall, own[number + 1], keep * own[number] + weight * (even + odd))
        minus = jnp.where(wall, own[number], keep * own[number + 1] + weight * (even - odd))
        if direction[2]:
            plus = pltpu.roll(plus, direction[2] % NZL, 1)
            minus = pltpu.roll(minus, -direction[2] % NZL, 1)
        yield number, plus
        yield number + 1, minus


BORDER = (13, 14, 15, 0, 1, 2, 3)


def border_kernel(
    omega_in, visible_in, levels_in, index_in, pop_in, solid_in,
    pop, solid, odd_message, even_message, shades,
    border, omega, visible, levels, index, sem,
):
    brick_x, brick_y = lax.axis_index("gx") * NXL // BRICK, lax.axis_index("gy") * NYL // BRICK
    pairs = [
        (omega_in, omega),
        (visible_in.at[brick_x], visible),
        (levels_in, levels),
        (index_in, index),
        (solid_in, solid),
    ]
    for i in range(NXL):
        rows = slice(i * NYL, (i + 1) * NYL)
        pairs.append((pop_in.at[:, rows, :], pop.at[:, rows, :]))
    copies = [pltpu.make_async_copy(source, target, sem.at[place]) for place, (source, target) in enumerate(pairs)]
    for copy in copies:
        copy.start()
    for copy in copies:
        copy.wait()
    rate = omega[0]
    lane = lax.broadcasted_iota(jnp.int32, (8, NZL), 1) // BRICK
    shown = jnp.zeros((8, NZL), jnp.int32)
    for brick in range(NZL // BRICK):
        shown = jnp.where(lane == brick, visible[brick, brick_y], shown)
    shades[0:8, :] = shown.astype(jnp.float32)
    shades[8:16, :] = jnp.full((8, NZL), levels[index[brick_x, brick_y]], jnp.float32)
    shades[16:24, :] = jnp.full((8, NZL), rate, jnp.float32)
    for place, row in enumerate(BORDER):
        rows = pl.ds(row, NXL, stride=NYL)
        own = [pop[number, rows, :] for number in range(19)]
        for number, tile in collided(own, solid[rows, :] == 1, rate):
            border[place, number] = tile

    def load(number, row):
        return border[BORDER.index(row), number]

    odd_place = lax.axis_index("gy") % 2 == 1

    @pl.when(odd_place)
    def _():
        pack_y(load, odd_message, UPWARD, NYL - 1, UP_ROWS)
        pack_y(load, even_message, DOWNWARD, 0, DOWN_ROWS)

    @pl.when(jnp.logical_not(odd_place))
    def _():
        pack_y(load, even_message, UPWARD, NYL - 1, UP_ROWS)
        pack_y(load, odd_message, DOWNWARD, 0, DOWN_ROWS)


def chooser(axis, even_message, odd_message):
    odd_place = lax.axis_index(axis) % 2 == 1

    def before(rows):
        return jnp.where(odd_place, even_message[rows, :], odd_message[rows, :])

    def after(rows):
        return jnp.where(odd_place, odd_message[rows, :], even_message[rows, :])

    return before, after


def shifted(tile, fill, step):
    row = lax.broadcasted_iota(jnp.int32, (NYL, NZL), 0)
    if step == 1:
        return jnp.where(row == 0, fill, pltpu.roll(tile, 1, 0))
    return jnp.where(row == NYL - 1, fill, pltpu.roll(tile, NYL - 1, 0))


def padded_at(layer, row):
    return (layer + 1) * PITCH + 8 + row


def inner_kernel(shades, pop, solid, passed, moments):
    rate = shades[16:17, :]

    def collide_layer(i, carry):
        rows = pl.ds(pl.multiple_of(i * NYL, NYL), NYL)
        own = [pop[number, rows, :] for number in range(19)]
        for number, tile in collided(own, solid[rows, :] == 1, rate):
            passed[number, rows, :] = tile
        return carry

    lax.fori_loop(0, NXL, collide_layer, 0)
    own_moments(passed, moments)


def flow_of(parts):
    inverse = 1.0 / parts[0]
    return [part * inverse for part in parts[1:]]


def put(message, at, values):
    for value in values:
        message[at : at + value.shape[0], :] = value
        at += value.shape[0]


def whole(moments, layer):
    at = padded_at(layer, 0)
    return [moments[which, at : at + NYL, :] for which in range(4)]


def pack_right_layers(moments, leaving, message):
    last = NXL - 1
    put(message, 0, flow_of(whole(moments, last - 1)))
    put(message, 48, whole(moments, last))
    put(message, 112, [leaving(number, last) for number in RIGHTWARD])


def pack_left_layers(moments, leaving, message):
    put(message, 0, whole(moments, 0))
    put(message, 64, flow_of(whole(moments, 1)) + flow_of(whole(moments, 2)))
    put(message, 160, [leaving(number, 0) for number in LEFTWARD])


X_RIGHT, X_LEFT = 192, 240


def own_moments(passed, moments):

    def source(number, layer):
        return passed[number, layer * NYL : (layer + 1) * NYL, :]

    def entering(numbers, signs, layer):
        tile = None
        for number, sign in zip(numbers, signs):
            tile = add(tile, source(number, layer), sign)
        return shifted(tile, 0.0, LATTICE[numbers[0]][1])

    def own_sums(layer):
        up = entering((3, 15, 17), (1, 1, 1), layer)
        down = entering((4, 16, 18), (1, 1, 1), layer)
        up_z = entering((15, 17), (1, -1), layer)
        down_z = entering((18, 16), (1, -1), layer)
        here5, here6 = source(5, layer), source(6, layer)
        return (source(0, layer) + here5 + here6 + up + down, up - down, here5 - here6 + up_z + down_z)

    def side_sums(layer, straight, plus, minus, rise, fall):
        moved_up = entering((plus,), (1,), layer)
        moved_down = entering((minus,), (1,), layer)
        a, b = source(rise, layer), source(fall, layer)
        return (source(straight, layer) + a + b + moved_up + moved_down, moved_up - moved_down, a - b)

    def to_right(layer):
        return side_sums(layer, 1, 7, 9, 11, 13)

    def to_left(layer):
        return side_sums(layer, 2, 10, 8, 14, 12)

    def store(layer, values):
        at = padded_at(layer, 0)
        for which in range(4):
            moments[which, at : at + NYL, :] = values[which]

    for layer in range(NXL):
        parts, along_x = list(own_sums(layer)), None
        if layer > 0:
            extra = to_right(layer - 1)
            parts, along_x = [p + q for p, q in zip(parts, extra)], extra[0]
        if layer < NXL - 1:
            extra = to_left(layer + 1)
            parts, along_x = [p + q for p, q in zip(parts, extra)], add(along_x, extra[0], -1)
        store(layer, (parts[0], along_x, parts[1], parts[2]))
    dens, along_y, along_z = to_left(0)
    store(-1, (dens, -dens, along_y, along_z))
    dens, along_y, along_z = to_right(NXL - 1)
    store(NXL, (dens, dens, along_y, along_z))
    for row in (-1, NYL):
        tiles, beyond, ahead = row_moments(lambda number, at: passed[number, pl.ds(at, NXL, stride=NYL), :], row)
        store_row(moments, row, tiles, beyond, ahead)


def store_row(moments, row, tiles, beyond, ahead):
    for which in range(4):
        moments[which, pl.ds(padded_at(0, row), NXL, stride=PITCH), :] = tiles[which]
    for layer, lines, sign in ((-1, ahead, -1), (NXL, beyond, 1)):
        at = padded_at(layer, row)
        for which, value in enumerate((lines[0], lines[0] if sign == 1 else -lines[0], lines[1], lines[2])):
            moments[which, at : at + 1, :] = value


def load_row(moments, row):
    tiles = [moments[which, pl.ds(padded_at(0, row), NXL, stride=PITCH), :] for which in range(4)]
    beyond, ahead = (
        [moments[which, padded_at(layer, row) : padded_at(layer, row) + 1, :] for which in (0, 2, 3)]
        for layer in (NXL, -1)
    )
    return tiles, beyond, ahead


def joining_kernel(passed, odd_in, even_in, moments_in, moments, odd_out, even_out):
    moments[...] = moments_in[...]
    before, after = chooser("gy", even_in, odd_in)
    low = {number: before(slice(8 * place, 8 * place + 8)) for place, number in enumerate(UPWARD)}
    high = {number: after(slice(8 * place, 8 * place + 8)) for place, number in enumerate(DOWNWARD)}

    def line_of(reader, at):
        return reader(slice(at, at + 1))

    def sums(first, second):
        return [[p + q for p, q in zip(a, b)] for a, b in zip(first, second)]

    edges = {}
    for row, lines in ((0, low), (NYL - 1, high)):
        store_row(moments, row, *sums(load_row(moments, row), tile_moments(lines)))
    for row in HALO_ROWS:
        reader, rows, place = (before, UP_ROWS, row + 2) if row < 0 else (after, DOWN_ROWS, row - 16)
        at = Y_MOMENTS + 32 * place
        tiles = [reader(slice(at + 8 * which, at + 8 * which + 8)) for which in range(4)]
        at = edge_start(rows) + 6 * place
        beyond = [line_of(reader, at + which) for which in range(3)]
        ahead = [line_of(reader, at + 3 + which) for which in range(3)]
        if row in (-1, 16):
            tiles, beyond, ahead = sums(load_row(moments, row), (tiles, beyond, ahead))
        store_row(moments, row, tiles, beyond, ahead)
        edges[row] = (tiles, beyond, ahead)

    def line(tiles, layer):
        return [tile[layer : layer + 1] for tile in tiles]

    def leaving(number, layer):
        tile = passed[number, layer * NYL : (layer + 1) * NYL, :]
        cy = LATTICE[number][1]
        if cy:
            tile = shifted(tile, (low if cy == 1 else high)[number][layer : layer + 1], cy)
        return tile

    def pack_right(message):
        last = NXL - 1
        pack_right_layers(moments, leaving, message)
        put(message, X_RIGHT, flow_of(line(edges[16][0], last - 1)) + line(edges[16][0], last) + [v for row in HALO_ROWS for v in edges[row][1]])

    def pack_left(message):
        pack_left_layers(moments, leaving, message)
        put(message, X_LEFT, [v for row in HALO_ROWS[:4] for v in line(edges[row][0], 0)] + flow_of(line(edges[16][0], 1)) + [v for row in HALO_ROWS for v in edges[row][2]])

    odd_place = lax.axis_index("gx") % 2 == 1

    @pl.when(odd_place)
    def _():
        pack_right(odd_out)
        pack_left(even_out)

    @pl.when(jnp.logical_not(odd_place))
    def _():
        pack_left(odd_out)
        pack_right(even_out)


BENT = tuple(number for number in range(19) if LATTICE[number][1])


def passing_kernel(passed, odd_in, even_in, moments, new, flow, moved, sem):
    copies = []

    def store(source, number):
        cx = LATTICE[number][0]
        rows = slice(max(0, cx) * NYL, (NXL + min(0, cx)) * NYL)
        copies.append(pltpu.make_async_copy(source, new.at[number, rows, :], sem.at[number]))
        copies[-1].start()

    for number, (cx, cy, _) in enumerate(LATTICE):
        if not cy:
            store(passed.at[number, max(0, -cx) * NYL : (NXL - max(0, cx)) * NYL, :], number)
    before, after = chooser("gy", even_in, odd_in)
    low = {number: before(slice(8 * place, 8 * place + 8)) for place, number in enumerate(UPWARD)}
    high = {number: after(slice(8 * place, 8 * place + 8)) for place, number in enumerate(DOWNWARD)}
    for place, number in enumerate(BENT):
        cx, cy, _ = LATTICE[number]
        lines = (low if cy == 1 else high)[number]
        for source in range(max(0, -cx), NXL - max(0, cx)):
            tile = passed[number, source * NYL : (source + 1) * NYL, :]
            target = (source + cx) * NYL
            moved[place, target : target + NYL, :] = shifted(tile, lines[source : source + 1], cy)
        store(moved.at[place, max(0, cx) * NYL : (NXL + min(0, cx)) * NYL, :], number)
    for layer in range(1, NXL - 1):
        at = padded_at(layer, -8)
        inverse = 1.0 / moments[0, at : at + PITCH, :]
        to = flow_at(layer, -8)
        for axis in range(3):
            flow[axis, to : to + PITCH, :] = moments[axis + 1, at : at + PITCH, :] * inverse
    for copy in copies:
        copy.wait()


def flow_at(layer, row):
    return (layer + 2) * PITCH + 8 + row


def result_kernel(
    shades, moments, inner_flow, odd_in, even_in, new_in,
    new, q_field, crossings,
    outer_flow, q_held, c_held, sem, out_sem,
):
    del new_in
    odd_place = lax.axis_index("gx") % 2 == 1

    def enters(message, start, numbers, layer, first):
        return [
            pltpu.make_async_copy(
                message.at[start + NYL * place : start + NYL * (place + 1), :],
                new.at[number, layer * NYL : (layer + 1) * NYL, :],
                sem.at[first + place],
            )
            for place, number in enumerate(numbers)
        ]

    def run(left_message, right_message):
        copied = enters(left_message, 112, RIGHTWARD, 0, 0) + enters(right_message, 160, LEFTWARD, NXL - 1, 5)
        for copy in copied:
            copy.start()
        copied += compute(left_message, right_message)
        for copy in copied:
            copy.wait()

    def stores(layer):
        rows = slice(layer * NYL, (layer + 2) * NYL)
        return [
            pltpu.make_async_copy(q_held.at[rows, :], q_field.at[rows, :], out_sem.at[0, layer // 2]),
            pltpu.make_async_copy(c_held.at[:, rows, :], crossings.at[:, rows, :], out_sem.at[1, layer // 2]),
        ]

    def flow_ref(layer):
        return inner_flow if 0 < layer < NXL - 1 else outer_flow

    def compute(left_message, right_message):
        flow = outer_flow
        started = []

        def store_flow(layer, row, parts):
            inverse = 1.0 / parts[0]
            at = flow_at(layer, row)
            for axis in range(3):
                flow[axis, at : at + parts[0].shape[0], :] = parts[axis + 1] * inverse

        def own(layer, row, size):
            at = padded_at(layer, row)
            return [moments[which, at : at + size, :] for which in range(4)]

        def both(first, second):
            return [p + q for p, q in zip(first, second)]

        def get(message, at, count, size):
            return [message[at + size * n : at + size * (n + 1), :] for n in range(count)]

        def signed(lines, sign):
            return [lines[0], lines[0] if sign == 1 else -lines[0], lines[1], lines[2]]

        for axis, value in enumerate(get(left_message, 0, 3, NYL)):
            flow[axis, flow_at(-2, 0) : flow_at(-2, NYL), :] = value
        for axis, value in enumerate(get(left_message, 192, 3, 1)):
            flow[axis, flow_at(-2, NYL) : flow_at(-2, NYL) + 1, :] = value
        store_flow(-1, 0, both(get(left_message, 48, 4, NYL), own(-1, 0, NYL)))
        store_flow(-1, NYL, both(get(left_message, 195, 4, 1), own(-1, NYL, 1)))
        n1, n7, n9, n11, n13 = get(left_message, 112, 5, NYL)
        store_flow(0, 0, both(signed([n1 + n7 + n9 + n11 + n13, n7 - n9, n11 - n13], 1), own(0, 0, NYL)))
        for place, row in enumerate(HALO_ROWS):
            store_flow(0, row, both(signed(get(left_message, 199 + 3 * place, 3, 1), 1), own(0, row, 1)))
        n2, n8, n10, n12, n14 = get(right_message, 160, 5, NYL)
        store_flow(NXL - 1, 0, both(signed([n2 + n8 + n10 + n12 + n14, n10 - n8, n14 - n12], -1), own(NXL - 1, 0, NYL)))
        for place, row in enumerate(HALO_ROWS):
            store_flow(NXL - 1, row, both(signed(get(right_message, 259 + 3 * place, 3, 1), -1), own(NXL - 1, row, 1)))
        store_flow(NXL, 0, both(get(right_message, 0, 4, NYL), own(NXL, 0, NYL)))
        for place, row in enumerate(HALO_ROWS[:4]):
            store_flow(NXL, row, both(get(right_message, 240 + 4 * place, 4, 1), own(NXL, row, 1)))
        for axis, value in enumerate(get(right_message, 64, 3, NYL)):
            flow[axis, flow_at(NXL + 1, 0) : flow_at(NXL + 1, NYL), :] = value
        for axis, value in enumerate(get(right_message, 256, 3, 1)):
            flow[axis, flow_at(NXL + 1, NYL) : flow_at(NXL + 1, NYL) + 1, :] = value
        for axis, value in enumerate(get(right_message, 112, 3, NYL)):
            flow[axis, flow_at(NXL + 2, 0) : flow_at(NXL + 2, NYL), :] = value

        def stencil(minus2, minus1, plus1, plus2):
            return 8.0 * (plus1 - minus1) + (minus2 - plus2)

        def scaled_at(load):
            grads = []
            for axis in range(3):
                centre = load(axis, 0, 0)
                grads.append(
                    (
                        stencil(*[load(axis, d, 0) for d in (-2, -1, 1, 2)]),
                        stencil(*[load(axis, 0, d) for d in (-2, -1, 1, 2)]),
                        stencil(*[pltpu.roll(centre, -d % NZL, 1) for d in (-2, -1, 1, 2)]),
                    )
                )
            inner = grads[0][0] * grads[0][0] + grads[1][1] * grads[1][1] + grads[2][2] * grads[2][2]
            inner = inner + 2.0 * (grads[0][1] * grads[1][0] + grads[0][2] * grads[2][0] + grads[1][2] * grads[2][1])
            return inner * (-50.0 / 144.0)

        def layer_load(layer):
            def load(axis, dx, dy):
                at = flow_at(layer + dx, dy)
                return flow_ref(layer + dx)[axis, at : at + NYL, :]

            return load

        lines = lax.broadcasted_iota(jnp.int32, (NXL, NZL), 0)

        def row_load(axis, dx, dy):
            rows = pl.ds(flow_at(dx, NYL + dy), NXL, stride=PITCH)
            inside = jnp.logical_and(lines + dx > 0, lines + dx < NXL - 1)
            return jnp.where(inside, inner_flow[axis, rows, :], outer_flow[axis, rows, :])

        shown = shades[0:1, :] > 0.5
        level = shades[8:9, :]

        def crossing(here, there):
            return jnp.where(shown, jnp.maximum(-here * there, 0.0) / (here * here + there * there + 0.25), 0.0)

        above = scaled_at(row_load)
        following = scaled_at(layer_load(0))
        for layer in range(NXL):
            scaled, following = following, scaled_at(layer_load(layer + 1))
            at = layer * NYL
            here = scaled - level
            q_held[at : at + NYL, :] = jnp.where(shown, scaled, 0.0)
            c_held[0, at : at + NYL, :] = crossing(here, following - level)
            c_held[1, at : at + NYL, :] = crossing(here, shifted(scaled, above[layer : layer + 1], -1) - level)
            c_held[2, at : at + NYL, :] = crossing(here, pltpu.roll(here, NZL - 1, 1))
            if layer % 2:
                for copy in stores(layer - 1):
                    copy.start()
                    started.append(copy)
        return started

    @pl.when(odd_place)
    def _():
        run(even_in, odd_in)

    @pl.when(jnp.logical_not(odd_place))
    def _():
        run(odd_in, even_in)


def swap(value, axis, parity):
    size = lax.axis_size(axis)
    pairs = []
    for i in range(size):
        mate = i + 1 if i % 2 == parity else i - 1
        pairs.append((i, mate % size))
    return lax.ppermute(value, axis, pairs)


VMEM = pl.BlockSpec(memory_space=pltpu.VMEM)
SMEM = pl.BlockSpec(memory_space=pltpu.SMEM)
ANY = pl.BlockSpec(memory_space=pl.ANY)
HBM = pl.BlockSpec(memory_space=pltpu.HBM)


def shape(*dims):
    return jax.ShapeDtypeStruct(dims, jnp.float32)


def held(*dims):
    return pltpu.VMEM(dims, jnp.float32)


LARGE = pltpu.CompilerParams(vmem_limit_bytes=61 << 20)
SMALL = pltpu.CompilerParams(vmem_limit_bytes=8 << 20)


def near(value):
    return pltpu.with_memory_space_constraint(value, pltpu.VMEM)


def per_device(populations, solid, visible, omega, iso_levels, iso_index):
    cells = NXL * NYL
    padded = (3, (NXL + 5) * PITCH, NZL)
    pop, solid, to_odd, to_even, shades = pl.pallas_call(
        border_kernel,
        out_shape=(
            held(19, cells, NZL),
            pltpu.VMEM((cells, NZL), jnp.int32),
            held(Y_LEN, NZL),
            held(Y_LEN, NZL),
            held(24, NZL),
        ),
        in_specs=[ANY] * 6,
        out_specs=(VMEM,) * 5,
        compiler_params=LARGE,
        scratch_shapes=[
            pltpu.VMEM((len(BORDER), 19, NXL, NZL), jnp.float32),
            pltpu.SMEM((1,), jnp.float32),
            pltpu.SMEM((NZL // BRICK, iso_index.shape[1]), jnp.int32),
            pltpu.SMEM((LEVELS,), jnp.float32),
            pltpu.SMEM(iso_index.shape, jnp.int32),
            pltpu.SemaphoreType.DMA((NXL + 5,)),
        ],
    )(omega, visible.transpose(0, 2, 1), iso_levels, iso_index, populations.reshape(19, cells, NZL), solid.reshape(cells, NZL))
    odd_y = near(swap(to_odd, "gy", 1))
    even_y = near(swap(to_even, "gy", 0))
    shades = near(shades)
    passed, moments = pl.pallas_call(
        inner_kernel,
        out_shape=(held(19, cells, NZL), held(4, (NXL + 2) * PITCH, NZL)),
        in_specs=[VMEM] * 3,
        out_specs=(VMEM,) * 2,
        compiler_params=SMALL,
    )(shades, near(pop), near(solid))
    passed = near(passed)
    moments, to_odd, to_even = pl.pallas_call(
        joining_kernel,
        out_shape=(held(4, (NXL + 2) * PITCH, NZL), held(X_LEN, NZL), held(X_LEN, NZL)),
        in_specs=[VMEM] * 4,
        out_specs=(VMEM,) * 3,
        compiler_params=SMALL,
    )(passed, odd_y, even_y, near(moments))
    moments = near(moments)
    odd_x = near(swap(to_odd, "gx", 1))
    even_x = near(swap(to_even, "gx", 0))
    new, flow = pl.pallas_call(
        passing_kernel,
        out_shape=(shape(19, cells, NZL), held(*padded)),
        in_specs=[VMEM] * 4,
        out_specs=(ANY, VMEM),
        compiler_params=SMALL,
        scratch_shapes=[pltpu.VMEM((len(BENT), cells, NZL), jnp.float32), pltpu.SemaphoreType.DMA((19,))],
    )(passed, odd_y, even_y, moments)
    new, q_field, crossings = pl.pallas_call(
        result_kernel,
        out_shape=(shape(19, cells, NZL), shape(cells, NZL), shape(3, cells, NZL)),
        in_specs=[VMEM] * 5 + [ANY],
        out_specs=(ANY,) * 3,
        compiler_params=SMALL,
        scratch_shapes=[
            pltpu.VMEM(padded, jnp.float32),
            pltpu.VMEM((cells, NZL), jnp.float32),
            pltpu.VMEM((3, cells, NZL), jnp.float32),
            pltpu.SemaphoreType.DMA((10,)),
            pltpu.SemaphoreType.DMA((2, NXL // 2)),
        ],
        input_output_aliases={5: 0},
    )(shades, moments, near(flow), odd_x, even_x, new)
    return (
        new.reshape(19, NXL, NYL, NZL),
        q_field.reshape(NXL, NYL, NZL),
        crossings.reshape(3, NXL, NYL, NZL),
    )


def solution(mesh):
    in_specs = (P(None, "gx", "gy", None), P("gx", "gy", None), P(), P(), P(), P())
    out_specs = (P(None, "gx", "gy", None), P("gx", "gy", None), P(None, "gx", "gy", None))
    return jax.shard_map(
        per_device, mesh=mesh, in_specs=in_specs, out_specs=out_specs, check_vma=False
    )
```

```python
import jax
import jax.numpy as jnp
from jax import lax
from jax.experimental import pallas as pl
from jax.experimental.pallas import tpu as pltpu
from jax.sharding import PartitionSpec as P

BRICK = 16
LEVELS = 8
NXL, NYL, NZL = 8, 16, 128

LATTICE = [
    (0, 0, 0),
    (1, 0, 0),
    (-1, 0, 0),
    (0, 1, 0),
    (0, -1, 0),
    (0, 0, 1),
    (0, 0, -1),
    (1, 1, 0),
    (-1, -1, 0),
    (1, -1, 0),
    (-1, 1, 0),
    (1, 0, 1),
    (-1, 0, -1),
    (1, 0, -1),
    (-1, 0, 1),
    (0, 1, 1),
    (0, -1, -1),
    (0, 1, -1),
    (0, -1, 1),
]
UPWARD = (3, 7, 10, 15, 17)
DOWNWARD = (4, 8, 9, 16, 18)
RIGHTWARD = (1, 7, 9, 11, 13)
LEFTWARD = (2, 8, 10, 12, 14)

Y_MOMENTS = 40
UP_ROWS = (14, 15)
DOWN_ROWS = (0, 1, 2)
Y_LEN = 160
X_LEN = 280
HALO_ROWS = (-2, -1, 16, 17, 18)
PITCH = 32


def edge_start(rows):
    return Y_MOMENTS + 32 * len(rows)


def add(total, value, sign=1):
    if total is None:
        return value if sign == 1 else -value
    return total + value if sign == 1 else total - value


def row_moments(load, row):
    return tile_moments(
        {number: load(number, row - cy) for number, (_, cy, _) in enumerate(LATTICE) if 0 <= row - cy < NYL}
    )


def tile_moments(tiles):
    dens, along_y, along_z = {}, {}, {}
    for number, (cx, cy, cz) in enumerate(LATTICE):
        if number in tiles:
            tile = tiles[number]
            dens[cx] = add(dens.get(cx), tile)
            if cy:
                along_y[cx] = add(along_y.get(cx), tile, cy)
            if cz:
                along_z[cx] = add(along_z.get(cx), tile, cz)
    layer = lax.broadcasted_iota(jnp.int32, (NXL, NZL), 0)
    zero = jnp.zeros((NXL, NZL), jnp.float32)

    def right(tile):
        return zero if tile is None else jnp.where(layer == 0, 0.0, pltpu.roll(tile, 1, 0))

    def left(tile):
        return zero if tile is None else jnp.where(layer == NXL - 1, 0.0, pltpu.roll(tile, NXL - 1, 0))

    def joined(parts):
        return (zero if parts.get(0) is None else parts[0]) + right(parts.get(1)) + left(parts.get(-1))

    tiles = (joined(dens), right(dens.get(1)) - left(dens.get(-1)), joined(along_y), joined(along_z))

    def line(tile, which):
        return jnp.zeros((1, NZL), jnp.float32) if tile is None else tile[which : which + 1]

    beyond = [line(part.get(1), NXL - 1) for part in (dens, along_y, along_z)]
    before = [line(part.get(-1), 0) for part in (dens, along_y, along_z)]
    return tiles, beyond, before


def pack_y(load, message, numbers, border, rows):
    for place, number in enumerate(numbers):
        message[8 * place : 8 * place + 8, :] = load(number, border)
    edge = edge_start(rows)
    for place, row in enumerate(rows):
        tiles, beyond, before = row_moments(load, row)
        for which in range(4):
            at = Y_MOMENTS + 32 * place + 8 * which
            message[at : at + 8, :] = tiles[which]
        for which in range(3):
            at = edge + 6 * place + which
            message[at : at + 1, :] = beyond[which]
            message[at + 3 : at + 4, :] = before[which]


PAIRS = ((1, (1, 0, 0)), (3, (0, 1, 0)), (5, (0, 0, 1)), (7, (1, 1, 0)), (9, (1, -1, 0)), (11, (1, 0, 1)), (13, (1, 0, -1)), (15, (0, 1, 1)), (17, (0, 1, -1)))


def combine(parts, direction):
    total = None
    for part, sign in zip(parts, direction):
        if sign:
            total = add(total, part, sign)
    return total


def collided(own, wall, rate):
    keep = 1.0 - rate
    differ = {number: own[number] - own[number + 1] for number, _ in PAIRS}
    density = own[0]
    for number, _ in PAIRS:
        density = density + (own[number] + own[number + 1])
    momentum = [combine([differ[number] for number, _ in PAIRS], [d[axis] for _, d in PAIRS]) for axis in range(3)]
    inverse = 1.0 / density
    velocity = [part * inverse for part in momentum]
    base = 1.0 - 1.5 * (velocity[0] * velocity[0] + velocity[1] * velocity[1] + velocity[2] * velocity[2])
    scale = rate * density
    weight1, weight2 = scale * (1.0 / 18.0), scale * (1.0 / 36.0)
    yield 0, jnp.where(wall, own[0], keep * own[0] + scale * (1.0 / 3.0) * base)
    for number, direction in PAIRS:
        along = combine(velocity, direction)
        weight = weight1 if number < 7 else weight2
        even = base + 4.5 * (along * along)
        odd = 3.0 * along
        plus = jnp.where(wall, own[number + 1], keep * own[number] + weight * (even + odd))
        minus = jnp.where(wall, own[number], keep * own[number + 1] + weight * (even - odd))
        if direction[2]:
            plus = pltpu.roll(plus, direction[2] % NZL, 1)
            minus = pltpu.roll(minus, -direction[2] % NZL, 1)
        yield number, plus
        yield number + 1, minus


BORDER = (13, 14, 15, 0, 1, 2, 3)


def unit_kernel(ones):
    ones[...] = jnp.ones((8, NZL), jnp.float32)


def border_kernel(omega, unit, pop, solid, odd_message, even_message, border):
    rate = unit[...] * omega[0]
    for place, row in enumerate(BORDER):
        rows = pl.ds(row, NXL, stride=NYL)
        own = [pop[number, rows, :] for number in range(19)]
        for number, tile in collided(own, solid[rows, :] == 1, rate):
            border[place, number] = tile

    def load(number, row):
        return border[BORDER.index(row), number]

    odd_place = lax.axis_index("gy") % 2 == 1

    @pl.when(odd_place)
    def _():
        pack_y(load, odd_message, UPWARD, NYL - 1, UP_ROWS)
        pack_y(load, even_message, DOWNWARD, 0, DOWN_ROWS)

    @pl.when(jnp.logical_not(odd_place))
    def _():
        pack_y(load, even_message, UPWARD, NYL - 1, UP_ROWS)
        pack_y(load, odd_message, DOWNWARD, 0, DOWN_ROWS)


def chooser(axis, even_message, odd_message):
    odd_place = lax.axis_index(axis) % 2 == 1

    def before(rows):
        return jnp.where(odd_place, even_message[rows, :], odd_message[rows, :])

    def after(rows):
        return jnp.where(odd_place, odd_message[rows, :], even_message[rows, :])

    return before, after


def shifted(tile, fill, step):
    row = lax.broadcasted_iota(jnp.int32, (NYL, NZL), 0)
    if step == 1:
        return jnp.where(row == 0, fill, pltpu.roll(tile, 1, 0))
    return jnp.where(row == NYL - 1, fill, pltpu.roll(tile, NYL - 1, 0))


def padded_at(layer, row):
    return (layer + 1) * PITCH + 8 + row


def inner_kernel(
    omega, unit, visible_in, levels_in, index_in, pop, solid,
    passed, moments, shades,
    visible, levels, index, sem,
):
    brick_x, brick_y = lax.axis_index("gx") * NXL // BRICK, lax.axis_index("gy") * NYL // BRICK
    pairs = ((visible_in.at[brick_x], visible), (levels_in, levels), (index_in, index))
    copies = [pltpu.make_async_copy(source, target, sem.at[place]) for place, (source, target) in enumerate(pairs)]
    for copy in copies:
        copy.start()
    rate = unit[0:1, :] * omega[0]

    def collide_layer(i, carry):
        rows = pl.ds(pl.multiple_of(i * NYL, NYL), NYL)
        own = [pop[number, rows, :] for number in range(19)]
        for number, tile in collided(own, solid[rows, :] == 1, rate):
            passed[number, rows, :] = tile
        return carry

    lax.fori_loop(0, NXL, collide_layer, 0)
    own_moments(passed, moments)
    for copy in copies:
        copy.wait()
    lane = lax.broadcasted_iota(jnp.int32, (8, NZL), 1) // BRICK
    shown = jnp.zeros((8, NZL), jnp.int32)
    for brick in range(NZL // BRICK):
        shown = jnp.where(lane == brick, visible[brick, brick_y], shown)
    shades[0:8, :] = shown.astype(jnp.float32)
    shades[8:16, :] = jnp.full((8, NZL), levels[index[brick_x, brick_y]], jnp.float32)


def flow_of(parts):
    inverse = 1.0 / parts[0]
    return [part * inverse for part in parts[1:]]


def put(message, at, values):
    for value in values:
        message[at : at + value.shape[0], :] = value
        at += value.shape[0]


def whole(moments, layer):
    at = padded_at(layer, 0)
    return [moments[which, at : at + NYL, :] for which in range(4)]


def pack_right_layers(moments, leaving, message):
    last = NXL - 1
    put(message, 0, flow_of(whole(moments, last - 1)))
    put(message, 48, whole(moments, last))
    put(message, 112, [leaving(number, last) for number in RIGHTWARD])


def pack_left_layers(moments, leaving, message):
    put(message, 0, whole(moments, 0))
    put(message, 64, flow_of(whole(moments, 1)) + flow_of(whole(moments, 2)))
    put(message, 160, [leaving(number, 0) for number in LEFTWARD])


X_RIGHT, X_LEFT = 192, 240


def own_moments(passed, moments):

    def source(number, layer):
        return passed[number, layer * NYL : (layer + 1) * NYL, :]

    def entering(numbers, signs, layer):
        tile = None
        for number, sign in zip(numbers, signs):
            tile = add(tile, source(number, layer), sign)
        return shifted(tile, 0.0, LATTICE[numbers[0]][1])

    def own_sums(layer):
        up = entering((3, 15, 17), (1, 1, 1), layer)
        down = entering((4, 16, 18), (1, 1, 1), layer)
        up_z = entering((15, 17), (1, -1), layer)
        down_z = entering((18, 16), (1, -1), layer)
        here5, here6 = source(5, layer), source(6, layer)
        return (source(0, layer) + here5 + here6 + up + down, up - down, here5 - here6 + up_z + down_z)

    def side_sums(layer, straight, plus, minus, rise, fall):
        moved_up = entering((plus,), (1,), layer)
        moved_down = entering((minus,), (1,), layer)
        a, b = source(rise, layer), source(fall, layer)
        return (source(straight, layer) + a + b + moved_up + moved_down, moved_up - moved_down, a - b)

    def to_right(layer):
        return side_sums(layer, 1, 7, 9, 11, 13)

    def to_left(layer):
        return side_sums(layer, 2, 10, 8, 14, 12)

    def store(layer, values):
        at = padded_at(layer, 0)
        for which in range(4):
            moments[which, at : at + NYL, :] = values[which]

    for layer in range(NXL):
        parts, along_x = list(own_sums(layer)), None
        if layer > 0:
            extra = to_right(layer - 1)
            parts, along_x = [p + q for p, q in zip(parts, extra)], extra[0]
        if layer < NXL - 1:
            extra = to_left(layer + 1)
            parts, along_x = [p + q for p, q in zip(parts, extra)], add(along_x, extra[0], -1)
        store(layer, (parts[0], along_x, parts[1], parts[2]))
    dens, along_y, along_z = to_left(0)
    store(-1, (dens, -dens, along_y, along_z))
    dens, along_y, along_z = to_right(NXL - 1)
    store(NXL, (dens, dens, along_y, along_z))
    for row in (-1, NYL):
        tiles, beyond, ahead = row_moments(lambda number, at: passed[number, pl.ds(at, NXL, stride=NYL), :], row)
        store_row(moments, row, tiles, beyond, ahead)


def store_row(moments, row, tiles, beyond, ahead):
    for which in range(4):
        moments[which, pl.ds(padded_at(0, row), NXL, stride=PITCH), :] = tiles[which]
    for layer, lines, sign in ((-1, ahead, -1), (NXL, beyond, 1)):
        at = padded_at(layer, row)
        for which, value in enumerate((lines[0], lines[0] if sign == 1 else -lines[0], lines[1], lines[2])):
            moments[which, at : at + 1, :] = value


def load_row(moments, row):
    tiles = [moments[which, pl.ds(padded_at(0, row), NXL, stride=PITCH), :] for which in range(4)]
    beyond, ahead = (
        [moments[which, padded_at(layer, row) : padded_at(layer, row) + 1, :] for which in (0, 2, 3)]
        for layer in (NXL, -1)
    )
    return tiles, beyond, ahead


def joining_kernel(passed, odd_in, even_in, moments_in, moments, odd_out, even_out):
    moments[...] = moments_in[...]
    before, after = chooser("gy", even_in, odd_in)
    low = {number: before(slice(8 * place, 8 * place + 8)) for place, number in enumerate(UPWARD)}
    high = {number: after(slice(8 * place, 8 * place + 8)) for place, number in enumerate(DOWNWARD)}

    def line_of(reader, at):
        return reader(slice(at, at + 1))

    def sums(first, second):
        return [[p + q for p, q in zip(a, b)] for a, b in zip(first, second)]

    edges = {}
    for row, lines in ((0, low), (NYL - 1, high)):
        store_row(moments, row, *sums(load_row(moments, row), tile_moments(lines)))
    for row in HALO_ROWS:
        reader, rows, place = (before, UP_ROWS, row + 2) if row < 0 else (after, DOWN_ROWS, row - 16)
        at = Y_MOMENTS + 32 * place
        tiles = [reader(slice(at + 8 * which, at + 8 * which + 8)) for which in range(4)]
        at = edge_start(rows) + 6 * place
        beyond = [line_of(reader, at + which) for which in range(3)]
        ahead = [line_of(reader, at + 3 + which) for which in range(3)]
        if row in (-1, 16):
            tiles, beyond, ahead = sums(load_row(moments, row), (tiles, beyond, ahead))
        store_row(moments, row, tiles, beyond, ahead)
        edges[row] = (tiles, beyond, ahead)

    def line(tiles, layer):
        return [tile[layer : layer + 1] for tile in tiles]

    def leaving(number, layer):
        tile = passed[number, layer * NYL : (layer + 1) * NYL, :]
        cy = LATTICE[number][1]
        if cy:
            tile = shifted(tile, (low if cy == 1 else high)[number][layer : layer + 1], cy)
        return tile

    def pack_right(message):
        last = NXL - 1
        pack_right_layers(moments, leaving, message)
        put(message, X_RIGHT, flow_of(line(edges[16][0], last - 1)) + line(edges[16][0], last) + [v for row in HALO_ROWS for v in edges[row][1]])

    def pack_left(message):
        pack_left_layers(moments, leaving, message)
        put(message, X_LEFT, [v for row in HALO_ROWS[:4] for v in line(edges[row][0], 0)] + flow_of(line(edges[16][0], 1)) + [v for row in HALO_ROWS for v in edges[row][2]])

    odd_place = lax.axis_index("gx") % 2 == 1

    @pl.when(odd_place)
    def _():
        pack_right(odd_out)
        pack_left(even_out)

    @pl.when(jnp.logical_not(odd_place))
    def _():
        pack_left(odd_out)
        pack_right(even_out)


BENT = tuple(number for number in range(19) if LATTICE[number][1])


def passing_kernel(passed, odd_in, even_in, moments, new, flow, moved, sem):
    copies = []

    def store(source, number):
        cx = LATTICE[number][0]
        rows = slice(max(0, cx) * NYL, (NXL + min(0, cx)) * NYL)
        copies.append(pltpu.make_async_copy(source, new.at[number, rows, :], sem.at[number]))
        copies[-1].start()

    for number, (cx, cy, _) in enumerate(LATTICE):
        if not cy:
            store(passed.at[number, max(0, -cx) * NYL : (NXL - max(0, cx)) * NYL, :], number)
    before, after = chooser("gy", even_in, odd_in)
    low = {number: before(slice(8 * place, 8 * place + 8)) for place, number in enumerate(UPWARD)}
    high = {number: after(slice(8 * place, 8 * place + 8)) for place, number in enumerate(DOWNWARD)}
    for place, number in enumerate(BENT):
        cx, cy, _ = LATTICE[number]
        lines = (low if cy == 1 else high)[number]
        for source in range(max(0, -cx), NXL - max(0, cx)):
            tile = passed[number, source * NYL : (source + 1) * NYL, :]
            target = (source + cx) * NYL
            moved[place, target : target + NYL, :] = shifted(tile, lines[source : source + 1], cy)
        store(moved.at[place, max(0, cx) * NYL : (NXL + min(0, cx)) * NYL, :], number)
    for layer in range(1, NXL - 1):
        at = padded_at(layer, -8)
        inverse = 1.0 / moments[0, at : at + PITCH, :]
        to = flow_at(layer, -8)
        for axis in range(3):
            flow[axis, to : to + PITCH, :] = moments[axis + 1, at : at + PITCH, :] * inverse
    for copy in copies:
        copy.wait()


def flow_at(layer, row):
    return (layer + 2) * PITCH + 8 + row


def result_kernel(
    shades, moments, inner_flow, odd_in, even_in, new_in,
    new, q_field, crossings,
    outer_flow, q_held, c_held, sem, out_sem,
):
    del new_in
    odd_place = lax.axis_index("gx") % 2 == 1

    def enters(message, start, numbers, layer, first):
        return [
            pltpu.make_async_copy(
                message.at[start + NYL * place : start + NYL * (place + 1), :],
                new.at[number, layer * NYL : (layer + 1) * NYL, :],
                sem.at[first + place],
            )
            for place, number in enumerate(numbers)
        ]

    def run(left_message, right_message):
        copied = enters(left_message, 112, RIGHTWARD, 0, 0) + enters(right_message, 160, LEFTWARD, NXL - 1, 5)
        for copy in copied:
            copy.start()
        copied += compute(left_message, right_message)
        for copy in copied:
            copy.wait()

    def stores(layer):
        rows = slice(layer * NYL, (layer + 2) * NYL)
        return [
            pltpu.make_async_copy(q_held.at[rows, :], q_field.at[rows, :], out_sem.at[0, layer // 2]),
            pltpu.make_async_copy(c_held.at[:, rows, :], crossings.at[:, rows, :], out_sem.at[1, layer // 2]),
        ]

    def flow_ref(layer):
        return inner_flow if 0 < layer < NXL - 1 else outer_flow

    def compute(left_message, right_message):
        flow = outer_flow
        started = []

        def store_flow(layer, row, parts):
            inverse = 1.0 / parts[0]
            at = flow_at(layer, row)
            for axis in range(3):
                flow[axis, at : at + parts[0].shape[0], :] = parts[axis + 1] * inverse

        def own(layer, row, size):
            at = padded_at(layer, row)
            return [moments[which, at : at + size, :] for which in range(4)]

        def both(first, second):
            return [p + q for p, q in zip(first, second)]

        def get(message, at, count, size):
            return [message[at + size * n : at + size * (n + 1), :] for n in range(count)]

        def signed(lines, sign):
            return [lines[0], lines[0] if sign == 1 else -lines[0], lines[1], lines[2]]

        for axis, value in enumerate(get(left_message, 0, 3, NYL)):
            flow[axis, flow_at(-2, 0) : flow_at(-2, NYL), :] = value
        for axis, value in enumerate(get(left_message, 192, 3, 1)):
            flow[axis, flow_at(-2, NYL) : flow_at(-2, NYL) + 1, :] = value
        store_flow(-1, 0, both(get(left_message, 48, 4, NYL), own(-1, 0, NYL)))
        store_flow(-1, NYL, both(get(left_message, 195, 4, 1), own(-1, NYL, 1)))
        n1, n7, n9, n11, n13 = get(left_message, 112, 5, NYL)
        store_flow(0, 0, both(signed([n1 + n7 + n9 + n11 + n13, n7 - n9, n11 - n13], 1), own(0, 0, NYL)))
        for place, row in enumerate(HALO_ROWS):
            store_flow(0, row, both(signed(get(left_message, 199 + 3 * place, 3, 1), 1), own(0, row, 1)))
        n2, n8, n10, n12, n14 = get(right_message, 160, 5, NYL)
        store_flow(NXL - 1, 0, both(signed([n2 + n8 + n10 + n12 + n14, n10 - n8, n14 - n12], -1), own(NXL - 1, 0, NYL)))
        for place, row in enumerate(HALO_ROWS):
            store_flow(NXL - 1, row, both(signed(get(right_message, 259 + 3 * place, 3, 1), -1), own(NXL - 1, row, 1)))
        store_flow(NXL, 0, both(get(right_message, 0, 4, NYL), own(NXL, 0, NYL)))
        for place, row in enumerate(HALO_ROWS[:4]):
            store_flow(NXL, row, both(get(right_message, 240 + 4 * place, 4, 1), own(NXL, row, 1)))
        for axis, value in enumerate(get(right_message, 64, 3, NYL)):
            flow[axis, flow_at(NXL + 1, 0) : flow_at(NXL + 1, NYL), :] = value
        for axis, value in enumerate(get(right_message, 256, 3, 1)):
            flow[axis, flow_at(NXL + 1, NYL) : flow_at(NXL + 1, NYL) + 1, :] = value
        for axis, value in enumerate(get(right_message, 112, 3, NYL)):
            flow[axis, flow_at(NXL + 2, 0) : flow_at(NXL + 2, NYL), :] = value

        def stencil(minus2, minus1, plus1, plus2):
            return 8.0 * (plus1 - minus1) + (minus2 - plus2)

        def scaled_at(load):
            grads = []
            for axis in range(3):
                centre = load(axis, 0, 0)
                grads.append(
                    (
                        stencil(*[load(axis, d, 0) for d in (-2, -1, 1, 2)]),
                        stencil(*[load(axis, 0, d) for d in (-2, -1, 1, 2)]),
                        stencil(*[pltpu.roll(centre, -d % NZL, 1) for d in (-2, -1, 1, 2)]),
                    )
                )
            inner = grads[0][0] * grads[0][0] + grads[1][1] * grads[1][1] + grads[2][2] * grads[2][2]
            inner = inner + 2.0 * (grads[0][1] * grads[1][0] + grads[0][2] * grads[2][0] + grads[1][2] * grads[2][1])
            return inner * (-50.0 / 144.0)

        def layer_load(layer):
            def load(axis, dx, dy):
                at = flow_at(layer + dx, dy)
                return flow_ref(layer + dx)[axis, at : at + NYL, :]

            return load

        lines = lax.broadcasted_iota(jnp.int32, (NXL, NZL), 0)

        def row_load(axis, dx, dy):
            rows = pl.ds(flow_at(dx, NYL + dy), NXL, stride=PITCH)
            inside = jnp.logical_and(lines + dx > 0, lines + dx < NXL - 1)
            return jnp.where(inside, inner_flow[axis, rows, :], outer_flow[axis, rows, :])

        shown = shades[0:1, :] > 0.5
        level = shades[8:9, :]

        def crossing(here, there):
            return jnp.where(shown, jnp.maximum(-here * there, 0.0) / (here * here + there * there + 0.25), 0.0)

        above = scaled_at(row_load)
        following = scaled_at(layer_load(0))
        for layer in range(NXL):
            scaled, following = following, scaled_at(layer_load(layer + 1))
            at = layer * NYL
            here = scaled - level
            q_held[at : at + NYL, :] = jnp.where(shown, scaled, 0.0)
            c_held[0, at : at + NYL, :] = crossing(here, following - level)
            c_held[1, at : at + NYL, :] = crossing(here, shifted(scaled, above[layer : layer + 1], -1) - level)
            c_held[2, at : at + NYL, :] = crossing(here, pltpu.roll(here, NZL - 1, 1))
            if layer % 2:
                for copy in stores(layer - 1):
                    copy.start()
                    started.append(copy)
        return started

    @pl.when(odd_place)
    def _():
        run(even_in, odd_in)

    @pl.when(jnp.logical_not(odd_place))
    def _():
        run(odd_in, even_in)


def swap(value, axis, parity):
    size = lax.axis_size(axis)
    pairs = []
    for i in range(size):
        mate = i + 1 if i % 2 == parity else i - 1
        pairs.append((i, mate % size))
    return lax.ppermute(value, axis, pairs)


VMEM = pl.BlockSpec(memory_space=pltpu.VMEM)
SMEM = pl.BlockSpec(memory_space=pltpu.SMEM)
ANY = pl.BlockSpec(memory_space=pl.ANY)
HBM = pl.BlockSpec(memory_space=pltpu.HBM)


def shape(*dims):
    return jax.ShapeDtypeStruct(dims, jnp.float32)


def held(*dims):
    return pltpu.VMEM(dims, jnp.float32)


SMALL = pltpu.CompilerParams(vmem_limit_bytes=8 << 20)


def near(value):
    return pltpu.with_memory_space_constraint(value, pltpu.VMEM)


def per_device(populations, solid, visible, omega, iso_levels, iso_index):
    cells = NXL * NYL
    padded = (3, (NXL + 5) * PITCH, NZL)
    unit = pl.pallas_call(
        unit_kernel,
        out_shape=held(8, NZL),
        in_specs=[],
        out_specs=VMEM,
        compiler_params=SMALL,
        cost_estimate=pl.CostEstimate(flops=1_000_000_000, transcendentals=0, bytes_accessed=4096),
    )()
    unit = near(unit)
    pop = near(populations.reshape(19, cells, NZL))
    solid = near(solid.reshape(cells, NZL))
    to_odd, to_even = pl.pallas_call(
        border_kernel,
        out_shape=(held(Y_LEN, NZL), held(Y_LEN, NZL)),
        in_specs=[SMEM, VMEM, VMEM, VMEM],
        out_specs=(VMEM,) * 2,
        compiler_params=SMALL,
        scratch_shapes=[pltpu.VMEM((len(BORDER), 19, NXL, NZL), jnp.float32)],
    )(omega, unit, pop, solid)
    odd_y = near(swap(to_odd, "gy", 1))
    even_y = near(swap(to_even, "gy", 0))
    passed, moments, shades = pl.pallas_call(
        inner_kernel,
        out_shape=(held(19, cells, NZL), held(4, (NXL + 2) * PITCH, NZL), held(16, NZL)),
        in_specs=[SMEM, VMEM, ANY, ANY, ANY, VMEM, VMEM],
        out_specs=(VMEM,) * 3,
        compiler_params=SMALL,
        scratch_shapes=[
            pltpu.SMEM((NZL // BRICK, iso_index.shape[1]), jnp.int32),
            pltpu.SMEM((LEVELS,), jnp.float32),
            pltpu.SMEM(iso_index.shape, jnp.int32),
            pltpu.SemaphoreType.DMA((3,)),
        ],
    )(omega, unit, visible.transpose(0, 2, 1), iso_levels, iso_index, pop, solid)
    shades = near(shades)
    passed = near(passed)
    moments, to_odd, to_even = pl.pallas_call(
        joining_kernel,
        out_shape=(held(4, (NXL + 2) * PITCH, NZL), held(X_LEN, NZL), held(X_LEN, NZL)),
        in_specs=[VMEM] * 4,
        out_specs=(VMEM,) * 3,
        compiler_params=SMALL,
    )(passed, odd_y, even_y, near(moments))
    moments = near(moments)
    odd_x = near(swap(to_odd, "gx", 1))
    even_x = near(swap(to_even, "gx", 0))
    new, flow = pl.pallas_call(
        passing_kernel,
        out_shape=(shape(19, cells, NZL), held(*padded)),
        in_specs=[VMEM] * 4,
        out_specs=(ANY, VMEM),
        compiler_params=SMALL,
        scratch_shapes=[pltpu.VMEM((len(BENT), cells, NZL), jnp.float32), pltpu.SemaphoreType.DMA((19,))],
    )(passed, odd_y, even_y, moments)
    new, q_field, crossings = pl.pallas_call(
        result_kernel,
        out_shape=(shape(19, cells, NZL), shape(cells, NZL), shape(3, cells, NZL)),
        in_specs=[VMEM] * 5 + [ANY],
        out_specs=(ANY,) * 3,
        compiler_params=SMALL,
        scratch_shapes=[
            pltpu.VMEM(padded, jnp.float32),
            pltpu.VMEM((cells, NZL), jnp.float32),
            pltpu.VMEM((3, cells, NZL), jnp.float32),
            pltpu.SemaphoreType.DMA((10,)),
            pltpu.SemaphoreType.DMA((2, NXL // 2)),
        ],
        input_output_aliases={5: 0},
    )(shades, moments, near(flow), odd_x, even_x, new)
    return (
        new.reshape(19, NXL, NYL, NZL),
        q_field.reshape(NXL, NYL, NZL),
        crossings.reshape(3, NXL, NYL, NZL),
    )


def solution(mesh):
    in_specs = (P(None, "gx", "gy", None), P("gx", "gy", None), P(), P(), P(), P())
    out_specs = (P(None, "gx", "gy", None), P("gx", "gy", None), P(None, "gx", "gy", None))
    return jax.shard_map(
        per_device, mesh=mesh, in_specs=in_specs, out_specs=out_specs, check_vma=False
    )
```

```python
import jax
import jax.numpy as jnp
from jax import lax
from jax.experimental import pallas as pl
from jax.experimental.pallas import tpu as pltpu
from jax.sharding import PartitionSpec as P

BRICK = 16
LEVELS = 8
NXL, NYL, NZL = 8, 16, 128

LATTICE = [
    (0, 0, 0),
    (1, 0, 0),
    (-1, 0, 0),
    (0, 1, 0),
    (0, -1, 0),
    (0, 0, 1),
    (0, 0, -1),
    (1, 1, 0),
    (-1, -1, 0),
    (1, -1, 0),
    (-1, 1, 0),
    (1, 0, 1),
    (-1, 0, -1),
    (1, 0, -1),
    (-1, 0, 1),
    (0, 1, 1),
    (0, -1, -1),
    (0, 1, -1),
    (0, -1, 1),
]
UPWARD = (3, 7, 10, 15, 17)
DOWNWARD = (4, 8, 9, 16, 18)
RIGHTWARD = (1, 7, 9, 11, 13)
LEFTWARD = (2, 8, 10, 12, 14)

Y_MOMENTS = 40
UP_ROWS = (14, 15)
DOWN_ROWS = (0, 1, 2)
Y_LEN = 160
X_LEN = 280
HALO_ROWS = (-2, -1, 16, 17, 18)
PITCH = 32


def edge_start(rows):
    return Y_MOMENTS + 32 * len(rows)


def add(total, value, sign=1):
    if total is None:
        return value if sign == 1 else -value
    return total + value if sign == 1 else total - value


def row_moments(load, row):
    return tile_moments(
        {number: load(number, row - cy) for number, (_, cy, _) in enumerate(LATTICE) if 0 <= row - cy < NYL}
    )


def tile_moments(tiles):
    dens, along_y, along_z = {}, {}, {}
    for number, (cx, cy, cz) in enumerate(LATTICE):
        if number in tiles:
            tile = tiles[number]
            dens[cx] = add(dens.get(cx), tile)
            if cy:
                along_y[cx] = add(along_y.get(cx), tile, cy)
            if cz:
                along_z[cx] = add(along_z.get(cx), tile, cz)
    layer = lax.broadcasted_iota(jnp.int32, (NXL, NZL), 0)
    zero = jnp.zeros((NXL, NZL), jnp.float32)

    def right(tile):
        return zero if tile is None else jnp.where(layer == 0, 0.0, pltpu.roll(tile, 1, 0))

    def left(tile):
        return zero if tile is None else jnp.where(layer == NXL - 1, 0.0, pltpu.roll(tile, NXL - 1, 0))

    def joined(parts):
        return (zero if parts.get(0) is None else parts[0]) + right(parts.get(1)) + left(parts.get(-1))

    tiles = (joined(dens), right(dens.get(1)) - left(dens.get(-1)), joined(along_y), joined(along_z))

    def line(tile, which):
        return jnp.zeros((1, NZL), jnp.float32) if tile is None else tile[which : which + 1]

    beyond = [line(part.get(1), NXL - 1) for part in (dens, along_y, along_z)]
    before = [line(part.get(-1), 0) for part in (dens, along_y, along_z)]
    return tiles, beyond, before


def pack_y(load, message, numbers, border, rows):
    for place, number in enumerate(numbers):
        message[8 * place : 8 * place + 8, :] = load(number, border)
    edge = edge_start(rows)
    for place, row in enumerate(rows):
        tiles, beyond, before = row_moments(load, row)
        for which in range(4):
            at = Y_MOMENTS + 32 * place + 8 * which
            message[at : at + 8, :] = tiles[which]
        for which in range(3):
            at = edge + 6 * place + which
            message[at : at + 1, :] = beyond[which]
            message[at + 3 : at + 4, :] = before[which]


PAIRS = ((1, (1, 0, 0)), (3, (0, 1, 0)), (5, (0, 0, 1)), (7, (1, 1, 0)), (9, (1, -1, 0)), (11, (1, 0, 1)), (13, (1, 0, -1)), (15, (0, 1, 1)), (17, (0, 1, -1)))


def combine(parts, direction):
    total = None
    for part, sign in zip(parts, direction):
        if sign:
            total = add(total, part, sign)
    return total


def collided(own, wall, rate):
    keep = 1.0 - rate
    differ = {number: own[number] - own[number + 1] for number, _ in PAIRS}
    density = own[0]
    for number, _ in PAIRS:
        density = density + (own[number] + own[number + 1])
    momentum = [combine([differ[number] for number, _ in PAIRS], [d[axis] for _, d in PAIRS]) for axis in range(3)]
    inverse = 1.0 / density
    velocity = [part * inverse for part in momentum]
    base = 1.0 - 1.5 * (velocity[0] * velocity[0] + velocity[1] * velocity[1] + velocity[2] * velocity[2])
    scale = rate * density
    weight1, weight2 = scale * (1.0 / 18.0), scale * (1.0 / 36.0)
    yield 0, jnp.where(wall, own[0], keep * own[0] + scale * (1.0 / 3.0) * base)
    for number, direction in PAIRS:
        along = combine(velocity, direction)
        weight = weight1 if number < 7 else weight2
        even = base + 4.5 * (along * along)
        odd = 3.0 * along
        plus = jnp.where(wall, own[number + 1], keep * own[number] + weight * (even + odd))
        minus = jnp.where(wall, own[number], keep * own[number + 1] + weight * (even - odd))
        if direction[2]:
            plus = pltpu.roll(plus, direction[2] % NZL, 1)
            minus = pltpu.roll(minus, -direction[2] % NZL, 1)
        yield number, plus
        yield number + 1, minus


BORDER = (13, 14, 15, 0, 1, 2, 3)


def unit_kernel(ones):
    ones[...] = jnp.ones((8, NZL), jnp.float32)


def border_kernel(omega, unit, pop, solid, odd_message, even_message, border):
    rate = unit[...] * omega[0]
    for place, row in enumerate(BORDER):
        rows = pl.ds(row, NXL, stride=NYL)
        own = [pop[number, rows, :] for number in range(19)]
        for number, tile in collided(own, solid[rows, :] == 1, rate):
            border[place, number] = tile

    def load(number, row):
        return border[BORDER.index(row), number]

    odd_place = lax.axis_index("gy") % 2 == 1

    @pl.when(odd_place)
    def _():
        pack_y(load, odd_message, UPWARD, NYL - 1, UP_ROWS)
        pack_y(load, even_message, DOWNWARD, 0, DOWN_ROWS)

    @pl.when(jnp.logical_not(odd_place))
    def _():
        pack_y(load, even_message, UPWARD, NYL - 1, UP_ROWS)
        pack_y(load, odd_message, DOWNWARD, 0, DOWN_ROWS)


def chooser(axis, even_message, odd_message):
    odd_place = lax.axis_index(axis) % 2 == 1

    def before(rows):
        return jnp.where(odd_place, even_message[rows, :], odd_message[rows, :])

    def after(rows):
        return jnp.where(odd_place, odd_message[rows, :], even_message[rows, :])

    return before, after


def shifted(tile, fill, step):
    row = lax.broadcasted_iota(jnp.int32, (NYL, NZL), 0)
    if step == 1:
        return jnp.where(row == 0, fill, pltpu.roll(tile, 1, 0))
    return jnp.where(row == NYL - 1, fill, pltpu.roll(tile, NYL - 1, 0))


def padded_at(layer, row):
    return (layer + 1) * PITCH + 8 + row


def inner_kernel(
    omega, unit, visible_in, levels_in, index_in, pop, solid,
    passed, moments, shades,
    visible, levels, index, sem,
):
    brick_x, brick_y = lax.axis_index("gx") * NXL // BRICK, lax.axis_index("gy") * NYL // BRICK
    pairs = ((visible_in.at[brick_x], visible), (levels_in, levels), (index_in, index))
    copies = [pltpu.make_async_copy(source, target, sem.at[place]) for place, (source, target) in enumerate(pairs)]
    for copy in copies:
        copy.start()
    rate = unit[0:1, :] * omega[0]

    def collide_layer(i, carry):
        rows = pl.ds(pl.multiple_of(i * NYL, NYL), NYL)
        own = [pop[number, rows, :] for number in range(19)]
        for number, tile in collided(own, solid[rows, :] == 1, rate):
            passed[number, rows, :] = tile
        return carry

    lax.fori_loop(0, NXL, collide_layer, 0)
    own_moments(passed, moments)
    for copy in copies:
        copy.wait()
    lane = lax.broadcasted_iota(jnp.int32, (8, NZL), 1) // BRICK
    shown = jnp.zeros((8, NZL), jnp.int32)
    for brick in range(NZL // BRICK):
        shown = jnp.where(lane == brick, visible[brick, brick_y], shown)
    shades[0:8, :] = shown.astype(jnp.float32)
    shades[8:16, :] = jnp.full((8, NZL), levels[index[brick_x, brick_y]], jnp.float32)


def flow_of(parts):
    inverse = 1.0 / parts[0]
    return [part * inverse for part in parts[1:]]


def put(message, at, values):
    for value in values:
        message[at : at + value.shape[0], :] = value
        at += value.shape[0]


def whole(moments, layer):
    at = padded_at(layer, 0)
    return [moments[which, at : at + NYL, :] for which in range(4)]


def pack_right_layers(moments, leaving, message):
    last = NXL - 1
    put(message, 0, flow_of(whole(moments, last - 1)))
    put(message, 48, whole(moments, last))
    put(message, 112, [leaving(number, last) for number in RIGHTWARD])


def pack_left_layers(moments, leaving, message):
    put(message, 0, whole(moments, 0))
    put(message, 64, flow_of(whole(moments, 1)) + flow_of(whole(moments, 2)))
    put(message, 160, [leaving(number, 0) for number in LEFTWARD])


X_RIGHT, X_LEFT = 192, 240


def own_moments(passed, moments):

    def source(number, layer):
        return passed[number, layer * NYL : (layer + 1) * NYL, :]

    def entering(numbers, signs, layer):
        tile = None
        for number, sign in zip(numbers, signs):
            tile = add(tile, source(number, layer), sign)
        return shifted(tile, 0.0, LATTICE[numbers[0]][1])

    def own_sums(layer):
        up = entering((3, 15, 17), (1, 1, 1), layer)
        down = entering((4, 16, 18), (1, 1, 1), layer)
        up_z = entering((15, 17), (1, -1), layer)
        down_z = entering((18, 16), (1, -1), layer)
        here5, here6 = source(5, layer), source(6, layer)
        return (source(0, layer) + here5 + here6 + up + down, up - down, here5 - here6 + up_z + down_z)

    def side_sums(layer, straight, plus, minus, rise, fall):
        moved_up = entering((plus,), (1,), layer)
        moved_down = entering((minus,), (1,), layer)
        a, b = source(rise, layer), source(fall, layer)
        return (source(straight, layer) + a + b + moved_up + moved_down, moved_up - moved_down, a - b)

    def to_right(layer):
        return side_sums(layer, 1, 7, 9, 11, 13)

    def to_left(layer):
        return side_sums(layer, 2, 10, 8, 14, 12)

    def store(layer, values):
        at = padded_at(layer, 0)
        for which in range(4):
            moments[which, at : at + NYL, :] = values[which]

    for layer in range(NXL):
        parts, along_x = list(own_sums(layer)), None
        if layer > 0:
            extra = to_right(layer - 1)
            parts, along_x = [p + q for p, q in zip(parts, extra)], extra[0]
        if layer < NXL - 1:
            extra = to_left(layer + 1)
            parts, along_x = [p + q for p, q in zip(parts, extra)], add(along_x, extra[0], -1)
        store(layer, (parts[0], along_x, parts[1], parts[2]))
    dens, along_y, along_z = to_left(0)
    store(-1, (dens, -dens, along_y, along_z))
    dens, along_y, along_z = to_right(NXL - 1)
    store(NXL, (dens, dens, along_y, along_z))
    for row in (-1, NYL):
        tiles, beyond, ahead = row_moments(lambda number, at: passed[number, pl.ds(at, NXL, stride=NYL), :], row)
        store_row(moments, row, tiles, beyond, ahead)


def store_row(moments, row, tiles, beyond, ahead):
    for which in range(4):
        moments[which, pl.ds(padded_at(0, row), NXL, stride=PITCH), :] = tiles[which]
    for layer, lines, sign in ((-1, ahead, -1), (NXL, beyond, 1)):
        at = padded_at(layer, row)
        for which, value in enumerate((lines[0], lines[0] if sign == 1 else -lines[0], lines[1], lines[2])):
            moments[which, at : at + 1, :] = value


def load_row(moments, row):
    tiles = [moments[which, pl.ds(padded_at(0, row), NXL, stride=PITCH), :] for which in range(4)]
    beyond, ahead = (
        [moments[which, padded_at(layer, row) : padded_at(layer, row) + 1, :] for which in (0, 2, 3)]
        for layer in (NXL, -1)
    )
    return tiles, beyond, ahead


def joining_kernel(passed, odd_in, even_in, moments_in, moments, odd_out, even_out):
    moments[...] = moments_in[...]
    before, after = chooser("gy", even_in, odd_in)
    low = {number: before(slice(8 * place, 8 * place + 8)) for place, number in enumerate(UPWARD)}
    high = {number: after(slice(8 * place, 8 * place + 8)) for place, number in enumerate(DOWNWARD)}

    def line_of(reader, at):
        return reader(slice(at, at + 1))

    def sums(first, second):
        return [[p + q for p, q in zip(a, b)] for a, b in zip(first, second)]

    edges = {}
    for row, lines in ((0, low), (NYL - 1, high)):
        store_row(moments, row, *sums(load_row(moments, row), tile_moments(lines)))
    for row in HALO_ROWS:
        reader, rows, place = (before, UP_ROWS, row + 2) if row < 0 else (after, DOWN_ROWS, row - 16)
        at = Y_MOMENTS + 32 * place
        tiles = [reader(slice(at + 8 * which, at + 8 * which + 8)) for which in range(4)]
        at = edge_start(rows) + 6 * place
        beyond = [line_of(reader, at + which) for which in range(3)]
        ahead = [line_of(reader, at + 3 + which) for which in range(3)]
        if row in (-1, 16):
            tiles, beyond, ahead = sums(load_row(moments, row), (tiles, beyond, ahead))
        store_row(moments, row, tiles, beyond, ahead)
        edges[row] = (tiles, beyond, ahead)

    def line(tiles, layer):
        return [tile[layer : layer + 1] for tile in tiles]

    def leaving(number, layer):
        tile = passed[number, layer * NYL : (layer + 1) * NYL, :]
        cy = LATTICE[number][1]
        if cy:
            tile = shifted(tile, (low if cy == 1 else high)[number][layer : layer + 1], cy)
        return tile

    def pack_right(message):
        last = NXL - 1
        pack_right_layers(moments, leaving, message)
        put(message, X_RIGHT, flow_of(line(edges[16][0], last - 1)) + line(edges[16][0], last) + [v for row in HALO_ROWS for v in edges[row][1]])

    def pack_left(message):
        pack_left_layers(moments, leaving, message)
        put(message, X_LEFT, [v for row in HALO_ROWS[:4] for v in line(edges[row][0], 0)] + flow_of(line(edges[16][0], 1)) + [v for row in HALO_ROWS for v in edges[row][2]])

    odd_place = lax.axis_index("gx") % 2 == 1

    @pl.when(odd_place)
    def _():
        pack_right(odd_out)
        pack_left(even_out)

    @pl.when(jnp.logical_not(odd_place))
    def _():
        pack_left(odd_out)
        pack_right(even_out)


BENT = tuple(number for number in range(19) if LATTICE[number][1])


def passing_kernel(passed, odd_in, even_in, moments, new, flow, parts, moved, sem):
    copies = []

    def store(source, number):
        cx = LATTICE[number][0]
        rows = slice(max(0, cx) * NYL, (NXL + min(0, cx)) * NYL)
        copies.append(pltpu.make_async_copy(source, new.at[number, rows, :], sem.at[number]))
        copies[-1].start()

    for number, (cx, cy, _) in enumerate(LATTICE):
        if not cy:
            store(passed.at[number, max(0, -cx) * NYL : (NXL - max(0, cx)) * NYL, :], number)
    before, after = chooser("gy", even_in, odd_in)
    low = {number: before(slice(8 * place, 8 * place + 8)) for place, number in enumerate(UPWARD)}
    high = {number: after(slice(8 * place, 8 * place + 8)) for place, number in enumerate(DOWNWARD)}
    for place, number in enumerate(BENT):
        cx, cy, _ = LATTICE[number]
        lines = (low if cy == 1 else high)[number]
        for source in range(max(0, -cx), NXL - max(0, cx)):
            tile = passed[number, source * NYL : (source + 1) * NYL, :]
            target = (source + cx) * NYL
            moved[place, target : target + NYL, :] = shifted(tile, lines[source : source + 1], cy)
        store(moved.at[place, max(0, cx) * NYL : (NXL + min(0, cx)) * NYL, :], number)
    for layer in range(1, NXL - 1):
        at = padded_at(layer, -8)
        inverse = 1.0 / moments[0, at : at + PITCH, :]
        to = flow_at(layer, -8)
        for axis in range(3):
            flow[axis, to : to + PITCH, :] = moments[axis + 1, at : at + PITCH, :] * inverse

    def layer_load(layer):
        def load(axis, dx, dy):
            at = flow_at(layer + dx, dy)
            return flow[axis, at : at + NYL, :]

        return load

    for layer in INNER:
        part = flat_part(layer_load(layer))
        rows = slice(layer * NYL, (layer + 1) * NYL)
        if layer in MIDDLE:
            parts[0, rows, :] = scaled_from(layer_load(layer), part)
        else:
            for which in range(3):
                parts[which, rows, :] = part[which]
    for copy in copies:
        copy.wait()


def flow_at(layer, row):
    return (layer + 2) * PITCH + 8 + row


def stencil(minus2, minus1, plus1, plus2):
    return 8.0 * (plus1 - minus1) + (minus2 - plus2)


def slopes(load, axis, second):
    if second == 0:
        return stencil(*[load(axis, d, 0) for d in (-2, -1, 1, 2)])
    if second == 1:
        return stencil(*[load(axis, 0, d) for d in (-2, -1, 1, 2)])
    centre = load(axis, 0, 0)
    return stencil(*[pltpu.roll(centre, -d % NZL, 1) for d in (-2, -1, 1, 2)])


def flat_part(load):
    g11, g22 = slopes(load, 1, 1), slopes(load, 2, 2)
    inner = g11 * g11 + g22 * g22 + 2.0 * (slopes(load, 1, 2) * slopes(load, 2, 1))
    return inner, slopes(load, 0, 1), slopes(load, 0, 2)


def scaled_from(load, part):
    inner, g01, g02 = part
    g00, g10, g20 = (slopes(load, axis, 0) for axis in range(3))
    return (g00 * g00 + inner + 2.0 * (g01 * g10 + g02 * g20)) * (-50.0 / 144.0)


INNER = range(1, NXL - 1)
MIDDLE = range(3, NXL - 3)


def result_kernel(
    shades, moments, inner_flow, parts, odd_in, even_in, new_in,
    new, q_field, crossings,
    outer_flow, q_held, c_held, sem, out_sem,
):
    del new_in
    odd_place = lax.axis_index("gx") % 2 == 1

    def enters(message, start, numbers, layer, first):
        return [
            pltpu.make_async_copy(
                message.at[start + NYL * place : start + NYL * (place + 1), :],
                new.at[number, layer * NYL : (layer + 1) * NYL, :],
                sem.at[first + place],
            )
            for place, number in enumerate(numbers)
        ]

    def run(left_message, right_message):
        copied = enters(left_message, 112, RIGHTWARD, 0, 0) + enters(right_message, 160, LEFTWARD, NXL - 1, 5)
        for copy in copied:
            copy.start()
        copied += compute(left_message, right_message)
        for copy in copied:
            copy.wait()

    def stores(layer):
        rows = slice(layer * NYL, (layer + 2) * NYL)
        return [
            pltpu.make_async_copy(q_held.at[rows, :], q_field.at[rows, :], out_sem.at[0, layer // 2]),
            pltpu.make_async_copy(c_held.at[:, rows, :], crossings.at[:, rows, :], out_sem.at[1, layer // 2]),
        ]

    def flow_ref(layer):
        return inner_flow if 0 < layer < NXL - 1 else outer_flow

    def compute(left_message, right_message):
        flow = outer_flow
        started = []

        def store_flow(layer, row, parts):
            inverse = 1.0 / parts[0]
            at = flow_at(layer, row)
            for axis in range(3):
                flow[axis, at : at + parts[0].shape[0], :] = parts[axis + 1] * inverse

        def own(layer, row, size):
            at = padded_at(layer, row)
            return [moments[which, at : at + size, :] for which in range(4)]

        def both(first, second):
            return [p + q for p, q in zip(first, second)]

        def get(message, at, count, size):
            return [message[at + size * n : at + size * (n + 1), :] for n in range(count)]

        def signed(lines, sign):
            return [lines[0], lines[0] if sign == 1 else -lines[0], lines[1], lines[2]]

        for axis, value in enumerate(get(left_message, 0, 3, NYL)):
            flow[axis, flow_at(-2, 0) : flow_at(-2, NYL), :] = value
        for axis, value in enumerate(get(left_message, 192, 3, 1)):
            flow[axis, flow_at(-2, NYL) : flow_at(-2, NYL) + 1, :] = value
        store_flow(-1, 0, both(get(left_message, 48, 4, NYL), own(-1, 0, NYL)))
        store_flow(-1, NYL, both(get(left_message, 195, 4, 1), own(-1, NYL, 1)))
        n1, n7, n9, n11, n13 = get(left_message, 112, 5, NYL)
        store_flow(0, 0, both(signed([n1 + n7 + n9 + n11 + n13, n7 - n9, n11 - n13], 1), own(0, 0, NYL)))
        for place, row in enumerate(HALO_ROWS):
            store_flow(0, row, both(signed(get(left_message, 199 + 3 * place, 3, 1), 1), own(0, row, 1)))
        n2, n8, n10, n12, n14 = get(right_message, 160, 5, NYL)
        store_flow(NXL - 1, 0, both(signed([n2 + n8 + n10 + n12 + n14, n10 - n8, n14 - n12], -1), own(NXL - 1, 0, NYL)))
        for place, row in enumerate(HALO_ROWS):
            store_flow(NXL - 1, row, both(signed(get(right_message, 259 + 3 * place, 3, 1), -1), own(NXL - 1, row, 1)))
        store_flow(NXL, 0, both(get(right_message, 0, 4, NYL), own(NXL, 0, NYL)))
        for place, row in enumerate(HALO_ROWS[:4]):
            store_flow(NXL, row, both(get(right_message, 240 + 4 * place, 4, 1), own(NXL, row, 1)))
        for axis, value in enumerate(get(right_message, 64, 3, NYL)):
            flow[axis, flow_at(NXL + 1, 0) : flow_at(NXL + 1, NYL), :] = value
        for axis, value in enumerate(get(right_message, 256, 3, 1)):
            flow[axis, flow_at(NXL + 1, NYL) : flow_at(NXL + 1, NYL) + 1, :] = value
        for axis, value in enumerate(get(right_message, 112, 3, NYL)):
            flow[axis, flow_at(NXL + 2, 0) : flow_at(NXL + 2, NYL), :] = value

        def layer_load(layer):
            def load(axis, dx, dy):
                at = flow_at(layer + dx, dy)
                return flow_ref(layer + dx)[axis, at : at + NYL, :]

            return load

        lines = lax.broadcasted_iota(jnp.int32, (NXL, NZL), 0)

        def row_load(axis, dx, dy):
            rows = pl.ds(flow_at(dx, NYL + dy), NXL, stride=PITCH)
            inside = jnp.logical_and(lines + dx > 0, lines + dx < NXL - 1)
            return jnp.where(inside, inner_flow[axis, rows, :], outer_flow[axis, rows, :])

        shown = shades[0:1, :] > 0.5
        level = shades[8:9, :]

        def crossing(here, there):
            return jnp.where(shown, jnp.maximum(-here * there, 0.0) / (here * here + there * there + 0.25), 0.0)

        def scaled_at(layer):
            load = layer_load(layer)
            rows = slice(layer * NYL, (layer + 1) * NYL)
            if layer in MIDDLE:
                return parts[0, rows, :]
            if layer in INNER:
                return scaled_from(load, [parts[which, rows, :] for which in range(3)])
            return scaled_from(load, flat_part(load))

        above = scaled_from(row_load, flat_part(row_load))
        following = scaled_at(0)
        for layer in range(NXL):
            scaled, following = following, scaled_at(layer + 1)
            at = layer * NYL
            here = scaled - level
            q_held[at : at + NYL, :] = jnp.where(shown, scaled, 0.0)
            c_held[0, at : at + NYL, :] = crossing(here, following - level)
            c_held[1, at : at + NYL, :] = crossing(here, shifted(scaled, above[layer : layer + 1], -1) - level)
            c_held[2, at : at + NYL, :] = crossing(here, pltpu.roll(here, NZL - 1, 1))
            if layer % 2:
                for copy in stores(layer - 1):
                    copy.start()
                    started.append(copy)
        return started

    @pl.when(odd_place)
    def _():
        run(even_in, odd_in)

    @pl.when(jnp.logical_not(odd_place))
    def _():
        run(odd_in, even_in)


def swap(value, axis, parity):
    size = lax.axis_size(axis)
    pairs = []
    for i in range(size):
        mate = i + 1 if i % 2 == parity else i - 1
        pairs.append((i, mate % size))
    return lax.ppermute(value, axis, pairs)


VMEM = pl.BlockSpec(memory_space=pltpu.VMEM)
SMEM = pl.BlockSpec(memory_space=pltpu.SMEM)
ANY = pl.BlockSpec(memory_space=pl.ANY)


def shape(*dims):
    return jax.ShapeDtypeStruct(dims, jnp.float32)


def held(*dims):
    return pltpu.VMEM(dims, jnp.float32)


SMALL = pltpu.CompilerParams(vmem_limit_bytes=8 << 20)


def near(value):
    return pltpu.with_memory_space_constraint(value, pltpu.VMEM)


def per_device(populations, solid, visible, omega, iso_levels, iso_index):
    cells = NXL * NYL
    padded = (3, (NXL + 5) * PITCH, NZL)
    unit = pl.pallas_call(
        unit_kernel,
        out_shape=held(8, NZL),
        in_specs=[],
        out_specs=VMEM,
        compiler_params=SMALL,
        cost_estimate=pl.CostEstimate(flops=1_000_000_000, transcendentals=0, bytes_accessed=4096),
    )()
    unit = near(unit)
    pop = near(populations.reshape(19, cells, NZL))
    solid = near(solid.reshape(cells, NZL))
    to_odd, to_even = pl.pallas_call(
        border_kernel,
        out_shape=(held(Y_LEN, NZL), held(Y_LEN, NZL)),
        in_specs=[SMEM, VMEM, VMEM, VMEM],
        out_specs=(VMEM,) * 2,
        compiler_params=SMALL,
        scratch_shapes=[pltpu.VMEM((len(BORDER), 19, NXL, NZL), jnp.float32)],
    )(omega, unit, pop, solid)
    odd_y = near(swap(to_odd, "gy", 1))
    even_y = near(swap(to_even, "gy", 0))
    passed, moments, shades = pl.pallas_call(
        inner_kernel,
        out_shape=(held(19, cells, NZL), held(4, (NXL + 2) * PITCH, NZL), held(16, NZL)),
        in_specs=[SMEM, VMEM, ANY, ANY, ANY, VMEM, VMEM],
        out_specs=(VMEM,) * 3,
        compiler_params=SMALL,
        scratch_shapes=[
            pltpu.SMEM((NZL // BRICK, iso_index.shape[1]), jnp.int32),
            pltpu.SMEM((LEVELS,), jnp.float32),
            pltpu.SMEM(iso_index.shape, jnp.int32),
            pltpu.SemaphoreType.DMA((3,)),
        ],
    )(omega, unit, visible.transpose(0, 2, 1), iso_levels, iso_index, pop, solid)
    shades = near(shades)
    passed = near(passed)
    moments, to_odd, to_even = pl.pallas_call(
        joining_kernel,
        out_shape=(held(4, (NXL + 2) * PITCH, NZL), held(X_LEN, NZL), held(X_LEN, NZL)),
        in_specs=[VMEM] * 4,
        out_specs=(VMEM,) * 3,
        compiler_params=SMALL,
    )(passed, odd_y, even_y, near(moments))
    moments = near(moments)
    odd_x = near(swap(to_odd, "gx", 1))
    even_x = near(swap(to_even, "gx", 0))
    new, flow, parts = pl.pallas_call(
        passing_kernel,
        out_shape=(shape(19, cells, NZL), held(*padded), held(3, cells, NZL)),
        in_specs=[VMEM] * 4,
        out_specs=(ANY, VMEM, VMEM),
        compiler_params=SMALL,
        scratch_shapes=[pltpu.VMEM((len(BENT), cells, NZL), jnp.float32), pltpu.SemaphoreType.DMA((19,))],
    )(passed, odd_y, even_y, moments)
    new, q_field, crossings = pl.pallas_call(
        result_kernel,
        out_shape=(shape(19, cells, NZL), shape(cells, NZL), shape(3, cells, NZL)),
        in_specs=[VMEM] * 6 + [ANY],
        out_specs=(ANY,) * 3,
        compiler_params=SMALL,
        scratch_shapes=[
            pltpu.VMEM(padded, jnp.float32),
            pltpu.VMEM((cells, NZL), jnp.float32),
            pltpu.VMEM((3, cells, NZL), jnp.float32),
            pltpu.SemaphoreType.DMA((10,)),
            pltpu.SemaphoreType.DMA((2, NXL // 2)),
        ],
        input_output_aliases={6: 0},
    )(shades, moments, near(flow), near(parts), odd_x, even_x, new)
    return (
        new.reshape(19, NXL, NYL, NZL),
        q_field.reshape(NXL, NYL, NZL),
        crossings.reshape(3, NXL, NYL, NZL),
    )


def solution(mesh):
    in_specs = (P(None, "gx", "gy", None), P("gx", "gy", None), P(), P(), P(), P())
    out_specs = (P(None, "gx", "gy", None), P("gx", "gy", None), P(None, "gx", "gy", None))
    return jax.shard_map(
        per_device, mesh=mesh, in_specs=in_specs, out_specs=out_specs, check_vma=False
    )
```

```python
import jax
import jax.numpy as jnp
from jax import lax
from jax.experimental import pallas as pl
from jax.experimental.pallas import tpu as pltpu
from jax.sharding import PartitionSpec as P

BRICK = 16
LEVELS = 8
NXL, NYL, NZL = 8, 16, 128

LATTICE = [
    (0, 0, 0),
    (1, 0, 0),
    (-1, 0, 0),
    (0, 1, 0),
    (0, -1, 0),
    (0, 0, 1),
    (0, 0, -1),
    (1, 1, 0),
    (-1, -1, 0),
    (1, -1, 0),
    (-1, 1, 0),
    (1, 0, 1),
    (-1, 0, -1),
    (1, 0, -1),
    (-1, 0, 1),
    (0, 1, 1),
    (0, -1, -1),
    (0, 1, -1),
    (0, -1, 1),
]
UPWARD = (3, 7, 10, 15, 17)
DOWNWARD = (4, 8, 9, 16, 18)
RIGHTWARD = (1, 7, 9, 11, 13)
LEFTWARD = (2, 8, 10, 12, 14)

Y_MOMENTS = 40
UP_ROWS = (14, 15)
DOWN_ROWS = (0, 1, 2)
Y_LEN = 160
X_LEN = 280
HALO_ROWS = (-2, -1, 16, 17, 18)
PITCH = 32


def edge_start(rows):
    return Y_MOMENTS + 32 * len(rows)


def add(total, value, sign=1):
    if total is None:
        return value if sign == 1 else -value
    return total + value if sign == 1 else total - value


def row_moments(load, row):
    return tile_moments(
        {number: load(number, row - cy) for number, (_, cy, _) in enumerate(LATTICE) if 0 <= row - cy < NYL}
    )


def tile_moments(tiles):
    dens, along_y, along_z = {}, {}, {}
    for number, (cx, cy, cz) in enumerate(LATTICE):
        if number in tiles:
            tile = tiles[number]
            dens[cx] = add(dens.get(cx), tile)
            if cy:
                along_y[cx] = add(along_y.get(cx), tile, cy)
            if cz:
                along_z[cx] = add(along_z.get(cx), tile, cz)
    layer = lax.broadcasted_iota(jnp.int32, (NXL, NZL), 0)
    zero = jnp.zeros((NXL, NZL), jnp.float32)

    def right(tile):
        return zero if tile is None else jnp.where(layer == 0, 0.0, pltpu.roll(tile, 1, 0))

    def left(tile):
        return zero if tile is None else jnp.where(layer == NXL - 1, 0.0, pltpu.roll(tile, NXL - 1, 0))

    def joined(parts):
        return (zero if parts.get(0) is None else parts[0]) + right(parts.get(1)) + left(parts.get(-1))

    tiles = (joined(dens), right(dens.get(1)) - left(dens.get(-1)), joined(along_y), joined(along_z))

    def line(tile, which):
        return jnp.zeros((1, NZL), jnp.float32) if tile is None else tile[which : which + 1]

    beyond = [line(part.get(1), NXL - 1) for part in (dens, along_y, along_z)]
    before = [line(part.get(-1), 0) for part in (dens, along_y, along_z)]
    return tiles, beyond, before


def pack_y(load, message, numbers, border, rows):
    for place, number in enumerate(numbers):
        message[8 * place : 8 * place + 8, :] = load(number, border)
    edge = edge_start(rows)
    for place, row in enumerate(rows):
        tiles, beyond, before = row_moments(load, row)
        for which in range(4):
            at = Y_MOMENTS + 32 * place + 8 * which
            message[at : at + 8, :] = tiles[which]
        for which in range(3):
            at = edge + 6 * place + which
            message[at : at + 1, :] = beyond[which]
            message[at + 3 : at + 4, :] = before[which]


PAIRS = ((1, (1, 0, 0)), (3, (0, 1, 0)), (5, (0, 0, 1)), (7, (1, 1, 0)), (9, (1, -1, 0)), (11, (1, 0, 1)), (13, (1, 0, -1)), (15, (0, 1, 1)), (17, (0, 1, -1)))


def combine(parts, direction):
    total = None
    for part, sign in zip(parts, direction):
        if sign:
            total = add(total, part, sign)
    return total


def collided(own, wall, rate):
    keep = 1.0 - rate
    differ = {number: own[number] - own[number + 1] for number, _ in PAIRS}
    density = own[0]
    for number, _ in PAIRS:
        density = density + (own[number] + own[number + 1])
    momentum = [combine([differ[number] for number, _ in PAIRS], [d[axis] for _, d in PAIRS]) for axis in range(3)]
    inverse = 1.0 / density
    velocity = [part * inverse for part in momentum]
    base = 1.0 - 1.5 * (velocity[0] * velocity[0] + velocity[1] * velocity[1] + velocity[2] * velocity[2])
    scale = rate * density
    weight1, weight2 = scale * (1.0 / 18.0), scale * (1.0 / 36.0)
    yield 0, jnp.where(wall, own[0], keep * own[0] + scale * (1.0 / 3.0) * base)
    for number, direction in PAIRS:
        along = combine(velocity, direction)
        weight = weight1 if number < 7 else weight2
        even = base + 4.5 * (along * along)
        odd = 3.0 * along
        plus = jnp.where(wall, own[number + 1], keep * own[number] + weight * (even + odd))
        minus = jnp.where(wall, own[number], keep * own[number + 1] + weight * (even - odd))
        if direction[2]:
            plus = pltpu.roll(plus, direction[2] % NZL, 1)
            minus = pltpu.roll(minus, -direction[2] % NZL, 1)
        yield number, plus
        yield number + 1, minus


BORDER = (13, 14, 15, 0, 1, 2, 3)


def unit_kernel(ones):
    ones[...] = jnp.ones((8, NZL), jnp.float32)


def needed(number, row):
    if (row == NYL - 1 and number in UPWARD) or (row == 0 and number in DOWNWARD):
        return True
    return row + LATTICE[number][1] in (UP_ROWS if row > NYL // 2 else DOWN_ROWS)


def border_kernel(omega, unit, pop, solid, odd_message, even_message, border):
    rate = unit[...] * omega[0]
    for place, row in enumerate(BORDER):
        rows = pl.ds(row, NXL, stride=NYL)
        own = [pop[number, rows, :] for number in range(19)]
        for number, tile in collided(own, solid[rows, :] == 1, rate):
            if needed(number, row):
                border[place, number] = tile

    def load(number, row):
        return border[BORDER.index(row), number]

    odd_place = lax.axis_index("gy") % 2 == 1

    @pl.when(odd_place)
    def _():
        pack_y(load, odd_message, UPWARD, NYL - 1, UP_ROWS)
        pack_y(load, even_message, DOWNWARD, 0, DOWN_ROWS)

    @pl.when(jnp.logical_not(odd_place))
    def _():
        pack_y(load, even_message, UPWARD, NYL - 1, UP_ROWS)
        pack_y(load, odd_message, DOWNWARD, 0, DOWN_ROWS)


def chooser(axis, even_message, odd_message):
    odd_place = lax.axis_index(axis) % 2 == 1

    def before(rows):
        return jnp.where(odd_place, even_message[rows, :], odd_message[rows, :])

    def after(rows):
        return jnp.where(odd_place, odd_message[rows, :], even_message[rows, :])

    return before, after


def shifted(tile, fill, step):
    row = lax.broadcasted_iota(jnp.int32, (NYL, NZL), 0)
    if step == 1:
        return jnp.where(row == 0, fill, pltpu.roll(tile, 1, 0))
    return jnp.where(row == NYL - 1, fill, pltpu.roll(tile, NYL - 1, 0))


def padded_at(layer, row):
    return (layer + 1) * PITCH + 8 + row


def inner_kernel(
    omega, unit, visible_in, levels_in, index_in, pop, solid,
    passed, moments, shades,
    visible, levels, index, sem,
):
    brick_x, brick_y = lax.axis_index("gx") * NXL // BRICK, lax.axis_index("gy") * NYL // BRICK
    pairs = ((visible_in.at[brick_x], visible), (levels_in, levels), (index_in, index))
    copies = [pltpu.make_async_copy(source, target, sem.at[place]) for place, (source, target) in enumerate(pairs)]
    for copy in copies:
        copy.start()
    rate = unit[0:1, :] * omega[0]

    def collide_layer(i, carry):
        rows = pl.ds(pl.multiple_of(i * NYL, NYL), NYL)
        own = [pop[number, rows, :] for number in range(19)]
        for number, tile in collided(own, solid[rows, :] == 1, rate):
            passed[number, rows, :] = tile
        return carry

    lax.fori_loop(0, NXL, collide_layer, 0)
    own_moments(passed, moments)
    for copy in copies:
        copy.wait()
    lane = lax.broadcasted_iota(jnp.int32, (8, NZL), 1) // BRICK
    shown = jnp.zeros((8, NZL), jnp.int32)
    for brick in range(NZL // BRICK):
        shown = jnp.where(lane == brick, visible[brick, brick_y], shown)
    shades[0:8, :] = shown.astype(jnp.float32)
    shades[8:16, :] = jnp.full((8, NZL), levels[index[brick_x, brick_y]], jnp.float32)


def flow_of(parts):
    inverse = 1.0 / parts[0]
    return [part * inverse for part in parts[1:]]


def put(message, at, values):
    for value in values:
        message[at : at + value.shape[0], :] = value
        at += value.shape[0]


def whole(moments, layer):
    at = padded_at(layer, 0)
    return [moments[which, at : at + NYL, :] for which in range(4)]


def pack_right_layers(moments, leaving, message):
    last = NXL - 1
    put(message, 0, flow_of(whole(moments, last - 1)))
    put(message, 48, whole(moments, last))
    put(message, 112, [leaving(number, last) for number in RIGHTWARD])


def pack_left_layers(moments, leaving, message):
    put(message, 0, whole(moments, 0))
    put(message, 64, flow_of(whole(moments, 1)) + flow_of(whole(moments, 2)))
    put(message, 160, [leaving(number, 0) for number in LEFTWARD])


X_RIGHT, X_LEFT = 192, 240


def own_moments(passed, moments):

    def source(number, layer):
        return passed[number, layer * NYL : (layer + 1) * NYL, :]

    def entering(numbers, signs, layer):
        tile = None
        for number, sign in zip(numbers, signs):
            tile = add(tile, source(number, layer), sign)
        return shifted(tile, 0.0, LATTICE[numbers[0]][1])

    def own_sums(layer):
        up = entering((3, 15, 17), (1, 1, 1), layer)
        down = entering((4, 16, 18), (1, 1, 1), layer)
        up_z = entering((15, 17), (1, -1), layer)
        down_z = entering((18, 16), (1, -1), layer)
        here5, here6 = source(5, layer), source(6, layer)
        return (source(0, layer) + here5 + here6 + up + down, up - down, here5 - here6 + up_z + down_z)

    def side_sums(layer, straight, plus, minus, rise, fall):
        moved_up = entering((plus,), (1,), layer)
        moved_down = entering((minus,), (1,), layer)
        a, b = source(rise, layer), source(fall, layer)
        return (source(straight, layer) + a + b + moved_up + moved_down, moved_up - moved_down, a - b)

    def to_right(layer):
        return side_sums(layer, 1, 7, 9, 11, 13)

    def to_left(layer):
        return side_sums(layer, 2, 10, 8, 14, 12)

    def store(layer, values):
        at = padded_at(layer, 0)
        for which in range(4):
            moments[which, at : at + NYL, :] = values[which]

    for layer in range(NXL):
        parts, along_x = list(own_sums(layer)), None
        if layer > 0:
            extra = to_right(layer - 1)
            parts, along_x = [p + q for p, q in zip(parts, extra)], extra[0]
        if layer < NXL - 1:
            extra = to_left(layer + 1)
            parts, along_x = [p + q for p, q in zip(parts, extra)], add(along_x, extra[0], -1)
        store(layer, (parts[0], along_x, parts[1], parts[2]))
    dens, along_y, along_z = to_left(0)
    store(-1, (dens, -dens, along_y, along_z))
    dens, along_y, along_z = to_right(NXL - 1)
    store(NXL, (dens, dens, along_y, along_z))
    for row in (-1, NYL):
        tiles, beyond, ahead = row_moments(lambda number, at: passed[number, pl.ds(at, NXL, stride=NYL), :], row)
        store_row(moments, row, tiles, beyond, ahead)


def store_row(moments, row, tiles, beyond, ahead):
    for which in range(4):
        moments[which, pl.ds(padded_at(0, row), NXL, stride=PITCH), :] = tiles[which]
    for layer, lines, sign in ((-1, ahead, -1), (NXL, beyond, 1)):
        at = padded_at(layer, row)
        for which, value in enumerate((lines[0], lines[0] if sign == 1 else -lines[0], lines[1], lines[2])):
            moments[which, at : at + 1, :] = value


def load_row(moments, row):
    tiles = [moments[which, pl.ds(padded_at(0, row), NXL, stride=PITCH), :] for which in range(4)]
    beyond, ahead = (
        [moments[which, padded_at(layer, row) : padded_at(layer, row) + 1, :] for which in (0, 2, 3)]
        for layer in (NXL, -1)
    )
    return tiles, beyond, ahead


def joining_kernel(passed, odd_in, even_in, moments_in, moments, odd_out, even_out):
    for layer in range(-1, NXL + 1):
        at = padded_at(layer, 0)
        moments[:, at : at + NYL, :] = moments_in[:, at : at + NYL, :]
    before, after = chooser("gy", even_in, odd_in)
    low = {number: before(slice(8 * place, 8 * place + 8)) for place, number in enumerate(UPWARD)}
    high = {number: after(slice(8 * place, 8 * place + 8)) for place, number in enumerate(DOWNWARD)}

    def line_of(reader, at):
        return reader(slice(at, at + 1))

    def sums(first, second):
        return [[p + q for p, q in zip(a, b)] for a, b in zip(first, second)]

    edges = {}
    for row, lines in ((0, low), (NYL - 1, high)):
        store_row(moments, row, *sums(load_row(moments, row), tile_moments(lines)))
    for row in HALO_ROWS:
        reader, rows, place = (before, UP_ROWS, row + 2) if row < 0 else (after, DOWN_ROWS, row - 16)
        at = Y_MOMENTS + 32 * place
        tiles = [reader(slice(at + 8 * which, at + 8 * which + 8)) for which in range(4)]
        at = edge_start(rows) + 6 * place
        beyond = [line_of(reader, at + which) for which in range(3)]
        ahead = [line_of(reader, at + 3 + which) for which in range(3)]
        if row in (-1, 16):
            tiles, beyond, ahead = sums(load_row(moments_in, row), (tiles, beyond, ahead))
        store_row(moments, row, tiles, beyond, ahead)
        edges[row] = (tiles, beyond, ahead)

    def line(tiles, layer):
        return [tile[layer : layer + 1] for tile in tiles]

    def leaving(number, layer):
        tile = passed[number, layer * NYL : (layer + 1) * NYL, :]
        cy = LATTICE[number][1]
        if cy:
            tile = shifted(tile, (low if cy == 1 else high)[number][layer : layer + 1], cy)
        return tile

    def pack_right(message):
        last = NXL - 1
        pack_right_layers(moments, leaving, message)
        put(message, X_RIGHT, flow_of(line(edges[16][0], last - 1)) + line(edges[16][0], last) + [v for row in HALO_ROWS for v in edges[row][1]])

    def pack_left(message):
        pack_left_layers(moments, leaving, message)
        put(message, X_LEFT, [v for row in HALO_ROWS[:4] for v in line(edges[row][0], 0)] + flow_of(line(edges[16][0], 1)) + [v for row in HALO_ROWS for v in edges[row][2]])

    odd_place = lax.axis_index("gx") % 2 == 1

    @pl.when(odd_place)
    def _():
        pack_right(odd_out)
        pack_left(even_out)

    @pl.when(jnp.logical_not(odd_place))
    def _():
        pack_left(odd_out)
        pack_right(even_out)


BENT = tuple(number for number in range(19) if LATTICE[number][1])


def passing_kernel(passed, odd_in, even_in, moments, new, flow, parts, moved, sem):
    copies = []

    def store(source, number):
        cx = LATTICE[number][0]
        rows = slice(max(0, cx) * NYL, (NXL + min(0, cx)) * NYL)
        copies.append(pltpu.make_async_copy(source, new.at[number, rows, :], sem.at[number]))
        copies[-1].start()

    for number, (cx, cy, _) in enumerate(LATTICE):
        if not cy:
            store(passed.at[number, max(0, -cx) * NYL : (NXL - max(0, cx)) * NYL, :], number)
    before, after = chooser("gy", even_in, odd_in)
    low = {number: before(slice(8 * place, 8 * place + 8)) for place, number in enumerate(UPWARD)}
    high = {number: after(slice(8 * place, 8 * place + 8)) for place, number in enumerate(DOWNWARD)}
    for place, number in enumerate(BENT):
        cx, cy, _ = LATTICE[number]
        lines = (low if cy == 1 else high)[number]
        for source in range(max(0, -cx), NXL - max(0, cx)):
            tile = passed[number, source * NYL : (source + 1) * NYL, :]
            target = (source + cx) * NYL
            moved[place, target : target + NYL, :] = shifted(tile, lines[source : source + 1], cy)
        store(moved.at[place, max(0, cx) * NYL : (NXL + min(0, cx)) * NYL, :], number)
    for layer in range(1, NXL - 1):
        at = padded_at(layer, -8)
        inverse = 1.0 / moments[0, at : at + PITCH, :]
        to = flow_at(layer, -8)
        for axis in range(3):
            flow[axis, to : to + PITCH, :] = moments[axis + 1, at : at + PITCH, :] * inverse

    def layer_load(layer):
        def load(axis, dx, dy):
            at = flow_at(layer + dx, dy)
            return flow[axis, at : at + NYL, :]

        return load

    for layer in INNER:
        part = flat_part(layer_load(layer))
        rows = slice(layer * NYL, (layer + 1) * NYL)
        if layer in MIDDLE:
            parts[0, rows, :] = scaled_from(layer_load(layer), part)
        else:
            for which in range(3):
                parts[which, rows, :] = part[which]
    for copy in copies:
        copy.wait()


def flow_at(layer, row):
    return (layer + 2) * PITCH + 8 + row


def stencil(minus2, minus1, plus1, plus2):
    return 8.0 * (plus1 - minus1) + (minus2 - plus2)


def slopes(load, axis, second):
    if second == 0:
        return stencil(*[load(axis, d, 0) for d in (-2, -1, 1, 2)])
    if second == 1:
        return stencil(*[load(axis, 0, d) for d in (-2, -1, 1, 2)])
    centre = load(axis, 0, 0)
    return stencil(*[pltpu.roll(centre, -d % NZL, 1) for d in (-2, -1, 1, 2)])


def flat_part(load):
    g11, g22 = slopes(load, 1, 1), slopes(load, 2, 2)
    inner = g11 * g11 + g22 * g22 + 2.0 * (slopes(load, 1, 2) * slopes(load, 2, 1))
    return inner, slopes(load, 0, 1), slopes(load, 0, 2)


def scaled_from(load, part):
    inner, g01, g02 = part
    g00, g10, g20 = (slopes(load, axis, 0) for axis in range(3))
    return (g00 * g00 + inner + 2.0 * (g01 * g10 + g02 * g20)) * (-50.0 / 144.0)


INNER = range(1, NXL - 1)
MIDDLE = range(3, NXL - 3)


def result_kernel(
    shades, moments, inner_flow, parts, odd_in, even_in, new_in,
    new, q_field, crossings,
    outer_flow, q_held, c_held, sem, out_sem,
):
    del new_in
    odd_place = lax.axis_index("gx") % 2 == 1

    def enters(message, start, numbers, layer, first):
        return [
            pltpu.make_async_copy(
                message.at[start + NYL * place : start + NYL * (place + 1), :],
                new.at[number, layer * NYL : (layer + 1) * NYL, :],
                sem.at[first + place],
            )
            for place, number in enumerate(numbers)
        ]

    def run(left_message, right_message):
        copied = enters(left_message, 112, RIGHTWARD, 0, 0) + enters(right_message, 160, LEFTWARD, NXL - 1, 5)
        for copy in copied:
            copy.start()
        copied += compute(left_message, right_message)
        for copy in copied:
            copy.wait()

    def stores(layer):
        rows = slice(layer * NYL, (layer + 2) * NYL)
        return [
            pltpu.make_async_copy(q_held.at[rows, :], q_field.at[rows, :], out_sem.at[0, layer // 2]),
            pltpu.make_async_copy(c_held.at[:, rows, :], crossings.at[:, rows, :], out_sem.at[1, layer // 2]),
        ]

    def flow_ref(layer):
        return inner_flow if 0 < layer < NXL - 1 else outer_flow

    def compute(left_message, right_message):
        flow = outer_flow
        started = []

        def store_flow(layer, row, parts):
            inverse = 1.0 / parts[0]
            at = flow_at(layer, row)
            for axis in range(3):
                flow[axis, at : at + parts[0].shape[0], :] = parts[axis + 1] * inverse

        def own(layer, row, size):
            at = padded_at(layer, row)
            return [moments[which, at : at + size, :] for which in range(4)]

        def both(first, second):
            return [p + q for p, q in zip(first, second)]

        def get(message, at, count, size):
            return [message[at + size * n : at + size * (n + 1), :] for n in range(count)]

        def signed(lines, sign):
            return [lines[0], lines[0] if sign == 1 else -lines[0], lines[1], lines[2]]

        for axis, value in enumerate(get(left_message, 0, 3, NYL)):
            flow[axis, flow_at(-2, 0) : flow_at(-2, NYL), :] = value
        for axis, value in enumerate(get(left_message, 192, 3, 1)):
            flow[axis, flow_at(-2, NYL) : flow_at(-2, NYL) + 1, :] = value
        store_flow(-1, 0, both(get(left_message, 48, 4, NYL), own(-1, 0, NYL)))
        store_flow(-1, NYL, both(get(left_message, 195, 4, 1), own(-1, NYL, 1)))
        n1, n7, n9, n11, n13 = get(left_message, 112, 5, NYL)
        store_flow(0, 0, both(signed([n1 + n7 + n9 + n11 + n13, n7 - n9, n11 - n13], 1), own(0, 0, NYL)))
        for place, row in enumerate(HALO_ROWS):
            store_flow(0, row, both(signed(get(left_message, 199 + 3 * place, 3, 1), 1), own(0, row, 1)))
        n2, n8, n10, n12, n14 = get(right_message, 160, 5, NYL)
        store_flow(NXL - 1, 0, both(signed([n2 + n8 + n10 + n12 + n14, n10 - n8, n14 - n12], -1), own(NXL - 1, 0, NYL)))
        for place, row in enumerate(HALO_ROWS):
            store_flow(NXL - 1, row, both(signed(get(right_message, 259 + 3 * place, 3, 1), -1), own(NXL - 1, row, 1)))
        store_flow(NXL, 0, both(get(right_message, 0, 4, NYL), own(NXL, 0, NYL)))
        for place, row in enumerate(HALO_ROWS[:4]):
            store_flow(NXL, row, both(get(right_message, 240 + 4 * place, 4, 1), own(NXL, row, 1)))
        for axis, value in enumerate(get(right_message, 64, 3, NYL)):
            flow[axis, flow_at(NXL + 1, 0) : flow_at(NXL + 1, NYL), :] = value
        for axis, value in enumerate(get(right_message, 256, 3, 1)):
            flow[axis, flow_at(NXL + 1, NYL) : flow_at(NXL + 1, NYL) + 1, :] = value
        for axis, value in enumerate(get(right_message, 112, 3, NYL)):
            flow[axis, flow_at(NXL + 2, 0) : flow_at(NXL + 2, NYL), :] = value

        def layer_load(layer):
            def load(axis, dx, dy):
                at = flow_at(layer + dx, dy)
                return flow_ref(layer + dx)[axis, at : at + NYL, :]

            return load

        lines = lax.broadcasted_iota(jnp.int32, (NXL, NZL), 0)

        def row_load(axis, dx, dy):
            rows = pl.ds(flow_at(dx, NYL + dy), NXL, stride=PITCH)
            inside = jnp.logical_and(lines + dx > 0, lines + dx < NXL - 1)
            return jnp.where(inside, inner_flow[axis, rows, :], outer_flow[axis, rows, :])

        shown = shades[0:1, :] > 0.5
        level = shades[8:9, :]

        def crossing(here, there):
            return jnp.where(shown, jnp.maximum(-here * there, 0.0) / (here * here + there * there + 0.25), 0.0)

        def scaled_at(layer):
            load = layer_load(layer)
            rows = slice(layer * NYL, (layer + 1) * NYL)
            if layer in MIDDLE:
                return parts[0, rows, :]
            if layer in INNER:
                return scaled_from(load, [parts[which, rows, :] for which in range(3)])
            return scaled_from(load, flat_part(load))

        above = scaled_from(row_load, flat_part(row_load))
        following = scaled_at(0)
        for layer in range(NXL):
            scaled, following = following, scaled_at(layer + 1)
            at = layer * NYL
            here = scaled - level
            q_held[at : at + NYL, :] = jnp.where(shown, scaled, 0.0)
            c_held[0, at : at + NYL, :] = crossing(here, following - level)
            c_held[1, at : at + NYL, :] = crossing(here, shifted(scaled, above[layer : layer + 1], -1) - level)
            c_held[2, at : at + NYL, :] = crossing(here, pltpu.roll(here, NZL - 1, 1))
            if layer % 2:
                for copy in stores(layer - 1):
                    copy.start()
                    started.append(copy)
        return started

    @pl.when(odd_place)
    def _():
        run(even_in, odd_in)

    @pl.when(jnp.logical_not(odd_place))
    def _():
        run(odd_in, even_in)


def swap(value, axis, parity):
    size = lax.axis_size(axis)
    pairs = []
    for i in range(size):
        mate = i + 1 if i % 2 == parity else i - 1
        pairs.append((i, mate % size))
    return lax.ppermute(value, axis, pairs)


VMEM = pl.BlockSpec(memory_space=pltpu.VMEM)
SMEM = pl.BlockSpec(memory_space=pltpu.SMEM)
ANY = pl.BlockSpec(memory_space=pl.ANY)


def shape(*dims):
    return jax.ShapeDtypeStruct(dims, jnp.float32)


def held(*dims):
    return pltpu.VMEM(dims, jnp.float32)


SMALL = pltpu.CompilerParams(vmem_limit_bytes=8 << 20)


def near(value):
    return pltpu.with_memory_space_constraint(value, pltpu.VMEM)


def per_device(populations, solid, visible, omega, iso_levels, iso_index):
    cells = NXL * NYL
    padded = (3, (NXL + 5) * PITCH, NZL)
    unit = pl.pallas_call(
        unit_kernel,
        out_shape=held(8, NZL),
        in_specs=[],
        out_specs=VMEM,
        compiler_params=SMALL,
        cost_estimate=pl.CostEstimate(flops=1_000_000_000, transcendentals=0, bytes_accessed=4096),
    )()
    unit = near(unit)
    pop = near(populations.reshape(19, cells, NZL))
    solid = near(solid.reshape(cells, NZL))
    to_odd, to_even = pl.pallas_call(
        border_kernel,
        out_shape=(held(Y_LEN, NZL), held(Y_LEN, NZL)),
        in_specs=[SMEM, VMEM, VMEM, VMEM],
        out_specs=(VMEM,) * 2,
        compiler_params=SMALL,
        scratch_shapes=[pltpu.VMEM((len(BORDER), 19, NXL, NZL), jnp.float32)],
    )(omega, unit, pop, solid)
    odd_y = near(swap(to_odd, "gy", 1))
    even_y = near(swap(to_even, "gy", 0))
    passed, moments, shades = pl.pallas_call(
        inner_kernel,
        out_shape=(held(19, cells, NZL), held(4, (NXL + 2) * PITCH, NZL), held(16, NZL)),
        in_specs=[SMEM, VMEM, ANY, ANY, ANY, VMEM, VMEM],
        out_specs=(VMEM,) * 3,
        compiler_params=SMALL,
        scratch_shapes=[
            pltpu.SMEM((NZL // BRICK, iso_index.shape[1]), jnp.int32),
            pltpu.SMEM((LEVELS,), jnp.float32),
            pltpu.SMEM(iso_index.shape, jnp.int32),
            pltpu.SemaphoreType.DMA((3,)),
        ],
    )(omega, unit, visible.transpose(0, 2, 1), iso_levels, iso_index, pop, solid)
    shades = near(shades)
    passed = near(passed)
    moments, to_odd, to_even = pl.pallas_call(
        joining_kernel,
        out_shape=(held(4, (NXL + 2) * PITCH, NZL), held(X_LEN, NZL), held(X_LEN, NZL)),
        in_specs=[VMEM] * 4,
        out_specs=(VMEM,) * 3,
        compiler_params=SMALL,
    )(passed, odd_y, even_y, near(moments))
    moments = near(moments)
    odd_x = near(swap(to_odd, "gx", 1))
    even_x = near(swap(to_even, "gx", 0))
    new, flow, parts = pl.pallas_call(
        passing_kernel,
        out_shape=(shape(19, cells, NZL), held(*padded), held(3, cells, NZL)),
        in_specs=[VMEM] * 4,
        out_specs=(ANY, VMEM, VMEM),
        compiler_params=SMALL,
        scratch_shapes=[pltpu.VMEM((len(BENT), cells, NZL), jnp.float32), pltpu.SemaphoreType.DMA((19,))],
    )(passed, odd_y, even_y, moments)
    new, q_field, crossings = pl.pallas_call(
        result_kernel,
        out_shape=(shape(19, cells, NZL), shape(cells, NZL), shape(3, cells, NZL)),
        in_specs=[VMEM] * 6 + [ANY],
        out_specs=(ANY,) * 3,
        compiler_params=SMALL,
        scratch_shapes=[
            pltpu.VMEM(padded, jnp.float32),
            pltpu.VMEM((cells, NZL), jnp.float32),
            pltpu.VMEM((3, cells, NZL), jnp.float32),
            pltpu.SemaphoreType.DMA((10,)),
            pltpu.SemaphoreType.DMA((2, NXL // 2)),
        ],
        input_output_aliases={6: 0},
    )(shades, moments, near(flow), near(parts), odd_x, even_x, new)
    return (
        new.reshape(19, NXL, NYL, NZL),
        q_field.reshape(NXL, NYL, NZL),
        crossings.reshape(3, NXL, NYL, NZL),
    )


def solution(mesh):
    in_specs = (P(None, "gx", "gy", None), P("gx", "gy", None), P(), P(), P(), P())
    out_specs = (P(None, "gx", "gy", None), P("gx", "gy", None), P(None, "gx", "gy", None))
    return jax.shard_map(
        per_device, mesh=mesh, in_specs=in_specs, out_specs=out_specs, check_vma=False
    )
```
